128 devices in a mesh: grp: 4 (over z), blk: 32 (over x, y, core).
Axes of the slice: x: 4, y: 4, z: 4, core: 2. Of those that a mesh axis runs over, the one named last changes fastest.
Arguments:
- barrier_scale: float32 [384, 1536], P(('grp', 'blk')), may hold values from 0.1 to 10
- regularizer: float32 [384, 768], P(('grp', 'blk')), may hold values from 0.5 to 1.5
- availability: float32 [384, 768], P(('grp', 'blk')), may hold values from 0.2 to 1
- block_rhs: float32 [384, 768], P(('grp', 'blk')), may hold values from -6 to 6
- primal: float32 [384, 1536], P(('grp', 'blk')), may hold values from -6 to 6
- link_mask: int32 [384, 128], P(('grp', 'blk')), may hold values 0 or 1
- counts: int32 [128], P(('grp', 'blk')), may hold values from 1 to 3, as said below
- constraints: bfloat16 [768, 1536], replicated, may hold values from -0.15625 to 0.15625
- border: float32 [768, 768], replicated, may hold values from -0.21875 to 0.21875
- link_out: float32 [128, 1536], replicated, may hold values from -0.15625 to 0.15625
- link_in: float32 [768, 128], replicated, may hold values from -0.5 to 0.5
- first_diag: float32 [768], replicated, may hold values from 5.12 to 51.2
- first_rhs: float32 [768], replicated, may hold values from -320 to 320
Outputs:
- block_step: float32 [384, 768], P(('grp', 'blk'))
- first_step: float32 [768], replicated
The draws below stay inside these ranges and needn't reach their ends.
Inputs may be any that keep to these rules, and one draw needn't show every extreme that they name: Device d holds its first counts[d] slots; slots from counts[d] on are empty and ignored. Devices 2k and 2k+1 together hold exactly 4 hours; some device holds exactly 3 and some exactly 1.
All inputs are finite; a program needn't handle non-finite values. No bound on the sum of `link_mask` on one device may be relied on, other than what follows from the above.
Results may differ from the reference program's by a relative error of at most 0.0013.
Values sent between devices are 32-bit elements; how exact they have to be, the bound alone decides.
No kernel may reach another device: no remote copies, remote signals or barrier semaphores. Data moves between devices by JAX's collectives and lax.ppermute only.
A program may use at most 128 MiB of HBM per device.

```python
import math
import jax
import jax.numpy as jnp
from jax import lax

NB = 768
NV = 1536
NL = 768
NK = 128
BPD = 2
CAP = 3
BLOCKS = 256
SLOTS = 384
DEVICES = 128


def draw_counts(key, part):
    pairs = DEVICES // 2
    first_key = jax.random.fold_in(key, 11)
    pick_key = jax.random.fold_in(key, 12)
    lower_counts = jax.random.randint(first_key, (pairs,), 1, 2 * BPD, dtype=jnp.int32)
    forced = jax.random.randint(pick_key, (), 0, pairs, dtype=jnp.int32)
    lower_counts = jnp.where(jnp.arange(pairs, dtype=jnp.int32) == forced, 1, lower_counts).astype(jnp.int32)
    paired = jnp.stack([lower_counts, 2 * BPD - lower_counts], axis=1)
    return paired.reshape((DEVICES,)).astype(jnp.int32)


def place_ends(drawn, stream_key, low, high):
    longest = drawn.shape.index(max(drawn.shape))
    spots = []
    for shift in (0, 1):
        where = [jax.random.randint(jax.random.fold_in(stream_key, axis), (), 0, length) for axis, length in enumerate(drawn.shape)]
        where[longest] = (where[longest] + shift) % drawn.shape[longest]
        spots.append(tuple(where))
    return drawn.at[spots[0]].set(low).at[spots[1]].set(high)


def level_of(rng, extent, pieces, low, largest):
    level, own = 1.0, jax.random.fold_in(rng, 6)
    for position, blocks in pieces:
        heights = jnp.exp(jax.random.uniform(jax.random.fold_in(own, position), (blocks,), jnp.float32, low / len(pieces), largest / len(pieces)))
        level = level * jnp.repeat(heights, extent[position] // blocks).reshape([-1 if axis == position else 1 for axis in range(len(extent))])
    return level


def scatter_about(stream_key, extent, deviation, bound, split=(), held_as=jnp.bfloat16):
    array = deviation * jax.random.normal(stream_key, extent, jnp.float32)
    if split:
        array = array * level_of(stream_key, extent, split, -0.22, 0.18)
    return jnp.clip(array, -bound, bound).astype(held_as)


def setup_inputs(seed: int = 0) -> dict:
    keys = jax.random.split(jax.random.key(seed), 14)
    return {
        "barrier_scale": jnp.clip(jnp.exp(math.log(10.0) - 4.6051702 * jax.random.uniform(keys[0], (SLOTS, NV), jnp.float32) ** level_of(keys[0], (SLOTS, NV), ((0, 128),), -0.2, 0.2)), 0.1, 10.0),
        "regularizer": jnp.clip(0.5 + 1.0 * jax.random.uniform(keys[1], (SLOTS, NB), jnp.float32) ** level_of(keys[1], (SLOTS, NB), ((0, 128),), -0.2, 0.2), 0.5, 1.5),
        "availability": jnp.clip(0.2 + 0.8 * jax.random.uniform(keys[2], (SLOTS, NB), jnp.float32) ** level_of(keys[2], (SLOTS, NB), ((0, 128),), -0.2, 0.2), 0.2, 1.0),
        "block_rhs": scatter_about(keys[3], (SLOTS, NB), 1.0, 6.0, ((0, 128),), jnp.float32),
        "primal": scatter_about(keys[4], (SLOTS, NV), 1.0, 6.0, ((0, 128),), jnp.float32),
        "link_mask": place_ends((jax.random.randint(keys[5], (SLOTS, NK), 0, 2) < 1).astype(jnp.int32), jax.random.fold_in(keys[5], 1), 0, 1),
        "counts": draw_counts(jax.random.fold_in(keys[13], 71), 0),
        "constraints": scatter_about(keys[7], (NB, NV), NV ** -0.5, 0.15625),
        "border": scatter_about(keys[8], (NB, NL), NB ** -0.5, 0.21875, (), jnp.float32),
        "link_out": scatter_about(keys[9], (NK, NV), NV ** -0.5, 0.15625, (), jnp.float32),
        "link_in": scatter_about(keys[10], (NB, NK), NK ** -0.5, 0.5, (), jnp.float32),
        "first_diag": jnp.clip(jnp.exp(jax.random.uniform(keys[11], (NL,), jnp.float32, math.log(5.12), math.log(51.2))), 5.12, 51.2),
        "first_rhs": scatter_about(keys[12], (NL,), (0.2 * BLOCKS), 320.0, (), jnp.float32),
    }


HIGHEST_PRECISION = lax.Precision.HIGHEST

def factor_block(scale_row, diag_row, constraints):
    scaled = (constraints.astype(jnp.float32) * scale_row[None, :]).astype(jnp.bfloat16)
    kkt = lax.dot_general(scaled.astype(jnp.float32), constraints.astype(jnp.float32), (((1,), (1,)), ((), ())), preferred_element_type=jnp.float32)
    kkt = kkt + jnp.diag(diag_row)
    return jnp.linalg.cholesky(kkt)

def schur_terms(barrier_scale, regularizer, availability, corrected, weights, constraints, border):
    first_width = border.shape[1]

    def accumulate(partial_sums, block_items):
        schur_part, first_grad = partial_sums
        scale_row, diag_row, avail_row, corrected_row, weight = block_items
        lower_factor = factor_block(scale_row, diag_row, constraints)
        solved = jax.scipy.linalg.solve_triangular(lower_factor, avail_row[:, None] * border, lower=True)
        reduced = jax.scipy.linalg.solve_triangular(lower_factor, corrected_row, lower=True)
        gram_term = lax.dot_general(solved.astype(jnp.float32), solved.astype(jnp.float32), (((0,), (0,)), ((), ())), precision=HIGHEST_PRECISION, preferred_element_type=jnp.float32)
        inner_term = lax.dot_general(solved.astype(jnp.float32), reduced.astype(jnp.float32), (((0,), (0,)), ((), ())), precision=HIGHEST_PRECISION, preferred_element_type=jnp.float32)
        return ((schur_part + weight * gram_term, first_grad + weight * inner_term), lower_factor)
    initial = (jnp.zeros((first_width, first_width), jnp.float32), jnp.zeros((first_width,), jnp.float32))
    (schur_part, first_grad), lowers = lax.scan(accumulate, initial, (barrier_scale, regularizer, availability, corrected, weights))
    return (schur_part, first_grad, lowers)

def back_solve(lowers, availability, corrected, coupled):

    def single(block_items):
        lower_factor, avail_row, corrected_row = block_items
        residual = corrected_row - avail_row * coupled
        halfway = jax.scipy.linalg.solve_triangular(lower_factor, residual, lower=True)
        return jax.scipy.linalg.solve_triangular(lower_factor, halfway, lower=True, trans=1)
    return lax.map(single, (lowers, availability, corrected))

def reference(barrier_scale, regularizer, availability, block_rhs, primal, link_mask, counts, constraints, border, link_out, link_in, first_diag, first_rhs):
    count_ends = jnp.cumsum(counts).astype(jnp.int32)
    count_starts = (count_ends - counts).astype(jnp.int32)
    hour_index = jnp.arange(BLOCKS, dtype=jnp.int32)
    owner_dev = jnp.sum((count_ends[None, :] <= hour_index[:, None]).astype(jnp.int32), axis=1).astype(jnp.int32)
    hour_rows = (owner_dev * CAP + hour_index - count_starts[owner_dev]).astype(jnp.int32)
    link_state = lax.dot_general(primal[hour_rows].astype(jnp.float32), link_out.astype(jnp.float32), (((1,), (1,)), ((), ())), precision=HIGHEST_PRECISION, preferred_element_type=jnp.float32)
    previous = jnp.concatenate([jnp.zeros((1, NK), jnp.float32), link_state[:-1]], axis=0)
    linked = link_mask[hour_rows].astype(jnp.float32) * previous
    corrected = block_rhs[hour_rows] + lax.dot_general(linked.astype(jnp.float32), link_in.astype(jnp.float32), (((1,), (1,)), ((), ())), precision=HIGHEST_PRECISION, preferred_element_type=jnp.float32)
    schur_part, first_grad, lowers = schur_terms(barrier_scale[hour_rows], regularizer[hour_rows], availability[hour_rows], corrected, jnp.ones((BLOCKS,), jnp.float32), constraints, border)
    schur_matrix = schur_part + jnp.diag(first_diag)
    schur_factor = jnp.linalg.cholesky(schur_matrix)
    first_step = jax.scipy.linalg.cho_solve((schur_factor, True), first_grad - first_rhs)
    coupled = jnp.dot(border.astype(jnp.float32), first_step.astype(jnp.float32), precision=HIGHEST_PRECISION, preferred_element_type=jnp.float32)
    solutions = back_solve(lowers, availability[hour_rows], corrected, coupled)
    block_step = jnp.zeros((SLOTS, NB), jnp.float32).at[hour_rows].set(solutions)
    return (block_step, first_step)
```

```python
import functools

import jax
import jax.numpy as jnp
from jax import lax
from jax.experimental import pallas as pl
from jax.experimental.pallas import tpu as pltpu
from jax.sharding import Mesh
from jax.sharding import PartitionSpec as P

GRP_BLK = ("grp", "blk_0", "blk_1", "blk_2")
CHIPS = ("grp", "blk_0", "blk_1")
CORE = "blk_2"
HOURS = 2
TILE = 128
PANEL = 8
HIGHEST = lax.Precision.HIGHEST
F32 = jnp.float32
BF16 = jnp.bfloat16


def lanes_of(x, k):
    return jnp.broadcast_to(x[:, k : k + 1], x.shape)


def row_of(x, j):
    return jnp.broadcast_to(x[j : j + 1, :], x.shape)


def invert_tiles(refs):
    shape = (PANEL, TILE)
    lane = lax.broadcasted_iota(jnp.int32, shape, 1)
    sub = lax.broadcasted_iota(jnp.int32, shape, 0)
    panels = TILE // PANEL
    for t in range(panels):
        lo = PANEL * t
        inside = (lane >= lo) & (lane < lo + PANEL)
        eye = lane == sub + lo
        for ref in refs:
            tile = ref[...]
            rows = tile[lo : lo + PANEL, :]
            cols = [lanes_of(rows, lo + j) for j in range(PANEL)]
            rows = jnp.where(inside, jnp.where(eye, 1.0, 0.0), rows)
            for j in range(PANEL):
                own = sub == j
                inverse = 1.0 / row_of(cols[j], j)
                pivot = row_of(rows, j) * inverse
                col = cols[j]
                rows = jnp.where(own, pivot, rows - col * pivot)
                for q in range(j + 1, PANEL):
                    c = row_of(cols[q], j) * inverse
                    cols[q] = jnp.where(own, c, cols[q] - col * c)
            spread = [row_of(rows, j) for j in range(PANEL)]
            for s in range(1, panels):
                i = PANEL * ((t + s) % panels)
                other = tile[i : i + PANEL, :]
                acc = jnp.where(inside, 0.0, other)
                for j in range(PANEL):
                    acc = acc - lanes_of(other, lo + j) * spread[j]
                ref[i : i + PANEL, :] = acc
            ref[lo : lo + PANEL, :] = rows


def split(x):
    hi = x.astype(BF16)
    return hi, (x - hi.astype(F32)).astype(BF16)


def dot3(a, b):
    ah, al = split(a)
    bh, bl = split(b)
    return jnp.dot(
        jnp.concatenate([ah, ah, al], 1),
        jnp.concatenate([bh, bl, bh], 0),
        preferred_element_type=F32,
    )


def dot3_nt(a, b):
    ah, al = split(a)
    bh, bl = split(b)
    return lax.dot_general(
        jnp.concatenate([ah, ah, al], 1),
        jnp.concatenate([bh, bl, bh], 1),
        (((1,), (1,)), ((), ())),
        preferred_element_type=F32,
    )


def sweep_inverse(mats, tiles):
    count, n, _ = mats.shape

    def step(k, carry):
        at = pl.multiple_of(k * TILE, TILE)
        here = pl.ds(at, TILE)
        for m in range(count):
            tiles[m][...] = mats[m, here, here]
        invert_tiles([tiles[m] for m in range(count)])
        row = lax.broadcasted_iota(jnp.int32, (n, TILE), 0)
        pivot_rows = (row >= at) & (row < at + TILE)
        for m in range(count):
            inverse = tiles[m][...]
            mats[m, here, here] = jnp.zeros((TILE, TILE), F32)
            scaled = dot3(inverse, mats[m, here, :])
            column = mats[m, :, here]
            mats[m, :, here] = jnp.zeros((n, TILE), F32)
            mats[m, here, :] = scaled
            mats[m, here, here] = inverse
            mats[m] = mats[m] - dot3(jnp.where(pivot_rows, 0.0, column), mats[m, here, :])
        return carry

    lax.fori_loop(0, n // TILE, step, 0)


def as_column(row):
    n = row.shape[1]
    eye = lax.broadcasted_iota(jnp.int32, (TILE, TILE), 0) == lax.broadcasted_iota(
        jnp.int32, (TILE, TILE), 1
    )
    parts = []
    for t in range(0, n, TILE):
        wide = jnp.broadcast_to(row[:, t : t + TILE], (TILE, TILE))
        parts.append(jnp.sum(jnp.where(eye, wide, 0.0), axis=1, keepdims=True))
    return jnp.concatenate(parts, axis=0)


def hours_kernel(
    scale, diag, avail, avail_col, corrected_col, constraints, border, border_t,
    inverses, packed, solved, scaled, coupled, *tiles,
):
    nb = border.shape[0]
    wide = 256
    eye = lax.broadcasted_iota(jnp.int32, (TILE, TILE), 0) == lax.broadcasted_iota(
        jnp.int32, (TILE, TILE), 1
    )
    nt = (((1,), (1,)), ((), ()))
    for m in range(HOURS):
        scaled[...] = (constraints[...].astype(F32) * scale[m : m + 1, :]).astype(BF16)
        for c in range(0, nb, wide):
            both = lax.dot_general(
                scaled[...], constraints[c : c + wide, :], nt, preferred_element_type=F32
            ) + lax.dot_general(
                constraints[...], scaled[c : c + wide, :], nt, preferred_element_type=F32
            )
            inverses[m, :, c : c + wide] = 0.5 * both
        for c in range(0, nb, TILE):
            block = inverses[m, c : c + TILE, c : c + TILE]
            extra = jnp.where(eye, diag[m : m + 1, c : c + TILE], 0.0)
            inverses[m, c : c + TILE, c : c + TILE] = block + extra
    sweep_inverse(inverses, tiles)
    total = jnp.zeros((1, nb), F32)
    for m in range(HOURS):
        y = jnp.sum(corrected_col[:, m : m + 1] * inverses[m], axis=0, keepdims=True)
        solved[m : m + 1, :] = y
        total = total + avail[m : m + 1, :] * y
    gradient = jnp.sum(as_column(total) * border[...], axis=0, keepdims=True)
    middle = jnp.zeros((nb, nb), F32)
    for m in range(HOURS):
        middle = middle + inverses[m] * avail_col[:, m : m + 1] * avail[m : m + 1, :]
    coupled[...] = dot3_nt(middle, border_t[...])
    row = 0
    for i in range(0, nb, TILE):
        part = dot3(border_t[i : i + TILE, :], coupled[:, : i + TILE])
        for j in range(0, i + TILE, TILE):
            packed[row : row + TILE, :] = part[:, j : j + TILE]
            row += TILE
    packed[row:, :] = jnp.zeros((packed.shape[0] - row, TILE), F32)
    for t in range(nb // TILE):
        packed[row + t : row + t + 1, :] = gradient[:, t * TILE : (t + 1) * TILE]


def finish_kernel(
    packed, first_diag, first_rhs, border, avail_col, inverses, solved,
    first_step, steps, schur, *tiles,
):
    nb = border.shape[0]
    eye = lax.broadcasted_iota(jnp.int32, (TILE, TILE), 0) == lax.broadcasted_iota(
        jnp.int32, (TILE, TILE), 1
    )
    row = 0
    for i in range(0, nb, TILE):
        for j in range(0, i + TILE, TILE):
            block = packed[row : row + TILE, :]
            row += TILE
            if i == j:
                block = block + jnp.where(eye, first_diag[:, i : i + TILE], 0.0)
            else:
                schur[0, j : j + TILE, i : i + TILE] = block.T
            schur[0, i : i + TILE, j : j + TILE] = block
    sweep_inverse(schur, tiles)
    gradient = jnp.concatenate(
        [packed[row + t : row + t + 1, :] for t in range(nb // TILE)], axis=1
    )
    rhs = as_column(gradient - first_rhs[...])
    x = jnp.sum(rhs * schur[0], axis=0, keepdims=True)
    first_step[...] = x
    v = jnp.sum(border[...] * x, axis=1, keepdims=True)
    for m in range(HOURS):
        w = avail_col[:, m : m + 1] * v
        steps[m : m + 1, :] = solved[m : m + 1, :] - jnp.sum(
            w * inverses[m], axis=0, keepdims=True
        )


PARAMS = pltpu.CompilerParams(vmem_limit_bytes=56 * 2**20)


def tile_scratch(count):
    return [pltpu.VMEM((TILE, TILE), F32) for _ in range(count)]


def summed_over_all(array):
    rows, width = array.shape
    half = rows // 2
    core = lax.axis_index(CORE)
    chips = lax.axis_size(CHIPS)
    pair = [(0, 1), (1, 0)]
    kept = lax.dynamic_slice_in_dim(array, core * half, half, 0)
    sent = lax.dynamic_slice_in_dim(array, (1 - core) * half, half, 0)
    mine = kept + lax.ppermute(sent, CORE, pair)
    pieces = mine.reshape(chips, half // chips, width)
    piece = lax.all_to_all(pieces, CHIPS, 0, 0, tiled=True).sum(axis=0)
    spread = jnp.broadcast_to(piece[None], (chips, *piece.shape))
    mine = lax.all_to_all(spread, CHIPS, 0, 0, tiled=True).reshape(half, width)
    other = lax.ppermute(mine, CORE, pair)
    first = core == 0
    return jnp.concatenate([jnp.where(first, mine, other), jnp.where(first, other, mine)], axis=0)


def on_device(
    barrier_scale, regularizer, availability, block_rhs, primal, link_mask, counts,
    constraints, border, link_out, link_in, first_diag, first_rhs,
):
    nb = border.shape[0]
    nk = link_in.shape[1]
    count = counts[0]
    second = lax.axis_index(CORE) == 1
    devices = lax.axis_size(GRP_BLK)
    pair = [(0, 1), (1, 0)]
    mask = link_mask.astype(F32)
    state = lax.dot_general(
        primal, link_out, (((1,), (1,)), ((), ())), precision=HIGHEST, preferred_element_type=F32
    )
    two, three = count >= 2, count == 3
    last = jnp.where(three, state[2], jnp.where(two, state[1], state[0]))
    incoming = lax.ppermute(last, GRP_BLK, [(d, d + 1) for d in range(devices - 1)])
    fields = jnp.concatenate([barrier_scale, regularizer, availability, block_rhs, mask], axis=1)
    lent = jnp.where(second, fields[0], fields[2])
    message = lax.ppermute(jnp.concatenate([lent, state[1]]), CORE, pair)
    borrowed, borrowed_state = message[:-nk], message[-nk:]
    early = jnp.where(two, jnp.where(second & three, fields[1], fields[0]), borrowed)
    early = jnp.where(second, early, fields[0])
    late = jnp.where(two, fields[1], borrowed)
    late = jnp.where(second, jnp.where(three, fields[2], jnp.where(two, fields[1], fields[0])), late)
    early_state = jnp.where(three, state[0], jnp.where(two, incoming, borrowed_state))
    early_state = jnp.where(second, early_state, incoming)
    late_state = jnp.where(three, state[1], jnp.where(two, state[0], incoming))
    late_state = jnp.where(second, late_state, state[0])
    work = jnp.stack([early, late])
    nv = barrier_scale.shape[1]
    scale, diag, avail, rhs, active = jnp.split(
        work, [nv, nv + nb, nv + 2 * nb, nv + 3 * nb], axis=1
    )
    linked = active * jnp.stack([early_state, late_state])
    corrected = rhs + lax.dot_general(
        linked, link_in, (((1,), (1,)), ((), ())), precision=HIGHEST, preferred_element_type=F32
    )
    avail_col = avail.T
    rows = -(-(nb // TILE * (nb // TILE + 1) // 2 * TILE + 8) // (devices * 8)) * devices * 8
    inverses, packed, solved = pl.pallas_call(
        hours_kernel,
        out_shape=(
            jax.ShapeDtypeStruct((HOURS, nb, nb), F32),
            jax.ShapeDtypeStruct((rows, TILE), F32),
            jax.ShapeDtypeStruct((HOURS, nb), F32),
        ),
        scratch_shapes=[pltpu.VMEM((nb, nv), BF16), pltpu.VMEM((nb, nb), F32), *tile_scratch(HOURS)],
        compiler_params=PARAMS,
        name="hours",
    )(scale, diag, avail, avail_col, corrected.T, constraints, border, border.T)
    total = summed_over_all(packed)
    first_step, steps = pl.pallas_call(
        finish_kernel,
        out_shape=(jax.ShapeDtypeStruct((1, nb), F32), jax.ShapeDtypeStruct((HOURS, nb), F32)),
        scratch_shapes=[pltpu.VMEM((1, nb, nb), F32), *tile_scratch(1)],
        compiler_params=PARAMS,
        name="finish",
    )(total, first_diag[None], first_rhs[None], border, avail_col, inverses, solved)
    returned = lax.ppermute(jnp.where(second, steps[0], steps[1]), CORE, pair)
    zero = jnp.zeros((nb,), F32)
    slot_0 = jnp.where(second, jnp.where(three, returned, jnp.where(two, steps[0], steps[1])), steps[0])
    slot_1 = jnp.where(two, jnp.where(second & three, steps[0], steps[1]), zero)
    slot_2 = jnp.where(three, jnp.where(second, steps[1], returned), zero)
    return jnp.stack([slot_0, slot_1, slot_2]), first_step[0]


def solution(mesh):
    split_mesh = Mesh(mesh.devices.reshape(mesh.shape["grp"], 4, 4, 2), GRP_BLK)
    whole = P(GRP_BLK, None)
    placed = (whole,) * 6 + (P(GRP_BLK),) + (P(),) * 6
    return jax.shard_map(
        on_device, mesh=split_mesh, in_specs=placed, out_specs=(whole, P()), check_vma=False
    )
```

```python
import functools

import jax
import jax.numpy as jnp
from jax import lax
from jax.experimental import pallas as pl
from jax.experimental.pallas import tpu as pltpu
from jax.sharding import Mesh
from jax.sharding import PartitionSpec as P

GRP_BLK = ("grp", "blk_0", "blk_1", "blk_2")
CHIPS = ("grp", "blk_0", "blk_1")
CORE = "blk_2"
HOURS = 2
TILE = 128
PANEL = 8
HIGHEST = lax.Precision.HIGHEST
CHUNK = 256
F32 = jnp.float32
BF16 = jnp.bfloat16
NT = (((1,), (1,)), ((), ()))


def lanes_of(x, k):
    return jnp.broadcast_to(x[:, k : k + 1], x.shape)


def row_of(x, j):
    return jnp.broadcast_to(x[j : j + 1, :], x.shape)


def invert_tiles(refs, reach, work=()):
    work = list(work)
    done = 0
    shape = (PANEL, TILE)
    lane = lax.broadcasted_iota(jnp.int32, shape, 1)
    sub = lax.broadcasted_iota(jnp.int32, shape, 0)
    panels = TILE // PANEL
    groups = reach // PANEL
    each = range(len(refs))
    for base in range(0, TILE, reach):
        parts = [
            [ref[base + PANEL * g : base + PANEL * (g + 1), :] for g in range(groups)]
            for ref in refs
        ]
        before = [ref[...] for ref in refs] if reach < TILE else None
        for t in range(groups):
            lo = base + PANEL * t
            inside = (lane >= lo) & (lane < lo + PANEL)
            eye = lane == sub + lo
            rows = [parts[m][t] for m in each]
            cols = [[lanes_of(rows[m], lo + j) for j in range(PANEL)] for m in each]
            rows = [jnp.where(inside, jnp.where(eye, 1.0, 0.0), rows[m]) for m in each]
            for j in range(PANEL):
                own = sub == j
                inverse = [1.0 / row_of(cols[m][j], j) for m in each]
                pivot = [row_of(rows[m], j) * inverse[m] for m in each]
                col = [cols[m][j] for m in each]
                for q in range(j + 1, PANEL):
                    for m in each:
                        c = row_of(cols[m][q], j) * inverse[m]
                        cols[m][q] = jnp.where(own, c, cols[m][q] - col[m] * c)
                rows = [jnp.where(own, pivot[m], rows[m] - col[m] * pivot[m]) for m in each]
            others = [(t + s) % groups for s in range(1, groups)]
            for m in each:
                spread = [row_of(rows[m], j) for j in range(PANEL)]
                acc = {i: jnp.where(inside, 0.0, parts[m][i]) for i in others}
                for i in others[:1]:
                    for j in range(PANEL):
                        acc[i] = acc[i] - lanes_of(parts[m][i], lo + j) * spread[j]
                for j in range(PANEL):
                    for i in others[1:]:
                        acc[i] = acc[i] - lanes_of(parts[m][i], lo + j) * spread[j]
                for i in others:
                    parts[m][i] = acc[i]
                parts[m][t] = rows[m]
            past = lo // PANEL + 1
            while done < len(work) and done * panels < past * len(work):
                work[done]()
                done += 1
        if reach == TILE:
            for m in each:
                for g in range(groups):
                    refs[m][PANEL * g : PANEL * (g + 1), :] = parts[m][g]
            continue
        wide = lax.broadcasted_iota(jnp.int32, (TILE, TILE), 1)
        tall = lax.broadcasted_iota(jnp.int32, (TILE, TILE), 0)
        own_lanes = (wide >= base) & (wide < base + reach)
        own_rows = (tall >= base) & (tall < base + reach)
        for m in each:
            block = list(parts[m])
            if base:
                block.insert(0, jnp.zeros((base, TILE), F32))
            if base + reach < TILE:
                block.append(jnp.zeros((TILE - base - reach, TILE), F32))
            block = jnp.concatenate(block, axis=0)
            bh, bl = split(block)
            xh, xl = split(before[m])
            change = mm(jnp.concatenate([xh, xl], 1), jnp.concatenate([bh, bh], 0)) + mm(xh, bl)
            rest = jnp.where(own_lanes, 0.0, before[m]) - change
            refs[m][...] = jnp.where(own_rows, block, rest)


def mm(a, b):
    return jnp.dot(a, b, preferred_element_type=F32)


def split(x):
    hi = x.astype(BF16)
    return hi, (x - hi.astype(F32)).astype(BF16)


def left(x):
    h, l = split(x)
    return jnp.concatenate([h, h, l], 1)


def right(x):
    h, l = split(x)
    return jnp.concatenate([h, l, h], 0)


def dot3(a, b):
    return mm(left(a), right(b))


def dot3_nt(a, b):
    h, l = split(b)
    return lax.dot_general(
        left(a), jnp.concatenate([h, l, h], 1), NT, preferred_element_type=F32
    )


def sweep_inverse(mats, tiles, columns, rows, reach, woven):
    count, n, _ = mats.shape
    each = range(count)
    last = n // TILE - 1

    def begin(k):
        at = pl.multiple_of(k * TILE, TILE)
        here = pl.ds(at, TILE)
        row = lax.broadcasted_iota(jnp.int32, (n, TILE), 0)
        pivot_rows = (row >= at) & (row < at + TILE)
        for m in each:
            inverse = tiles[m][...]
            scaled = dot3(inverse, mats[m, here, :])
            columns[m] = left(jnp.where(pivot_rows, 0.0, mats[m, :, here]))
            mats[m, :, here] = jnp.zeros((n, TILE), F32)
            mats[m, here, :] = scaled
            mats[m, here, here] = inverse
            rows[m] = right(mats[m, here, :])

    def update(m, c):
        at = slice(c, c + CHUNK)
        mats[m, :, at] = mats[m, :, at] - mm(columns[m], rows[m, :, at])

    work = [functools.partial(update, m, c) for c in range(0, n, CHUNK) for m in each]

    def step(k, carry):
        begin(k)
        after = pl.ds(pl.multiple_of((k + 1) * TILE, TILE), TILE)
        for m in each:
            tiles[m][...] = mats[m, after, after] - mm(columns[m, after, :], rows[m, :, after])
        invert_tiles([tiles[m] for m in each], reach, work if woven else ())
        if not woven:
            for item in work:
                item()
        return carry

    for m in each:
        tiles[m][...] = mats[m, :TILE, :TILE]
    invert_tiles([tiles[m] for m in each], reach)
    lax.fori_loop(0, last, step, 0)
    begin(last)
    for item in work:
        item()


def as_column(row):
    n = row.shape[1]
    eye = lax.broadcasted_iota(jnp.int32, (TILE, TILE), 0) == lax.broadcasted_iota(
        jnp.int32, (TILE, TILE), 1
    )
    parts = []
    for t in range(0, n, TILE):
        wide = jnp.broadcast_to(row[:, t : t + TILE], (TILE, TILE))
        parts.append(jnp.sum(jnp.where(eye, wide, 0.0), axis=1, keepdims=True))
    return jnp.concatenate(parts, axis=0)


def diagonal():
    return lax.broadcasted_iota(jnp.int32, (TILE, TILE), 0) == lax.broadcasted_iota(
        jnp.int32, (TILE, TILE), 1
    )


def hours_kernel(
    place, barrier_scale, regularizer, availability, block_rhs, link_mask, state, incoming, message,
    link_in, constraints, border_hbm, border_t_hbm,
    inverses_hbm, packed, solved, avail,
    inverses, border, border_t, scaled, coupled, columns, rows, sems, *tiles,
):
    nb, nv = constraints.shape
    nk = link_in.shape[1]
    loads = [
        pltpu.make_async_copy(border_hbm, border, sems.at[0]),
        pltpu.make_async_copy(border_t_hbm, border_t, sems.at[1]),
    ]
    for load in loads:
        load.start()
    count, second = place[0], place[1] == 1
    two, three = count >= 2, count == 3
    eye = diagonal()

    def early_late(field, at):
        own = [field[s : s + 1, :].astype(F32) for s in range(3)]
        borrowed = message[:, at : at + field.shape[1]]
        early = jnp.where(two, jnp.where(second & three, own[1], own[0]), borrowed)
        early = jnp.where(second, early, own[0])
        late = jnp.where(three, own[2], jnp.where(two, own[1], own[0]))
        late = jnp.where(second, late, jnp.where(two, own[1], borrowed))
        return early, late

    scale = early_late(barrier_scale, 0)
    diag = early_late(regularizer, nv)
    for m in range(HOURS):
        scaled[...] = (constraints[...].astype(F32) * scale[m]).astype(BF16)
        for c in range(0, nb, CHUNK):
            both = lax.dot_general(
                scaled[...], constraints[c : c + CHUNK, :], NT, preferred_element_type=F32
            ) + lax.dot_general(
                constraints[...], scaled[c : c + CHUNK, :], NT, preferred_element_type=F32
            )
            inverses[m, :, c : c + CHUNK] = 0.5 * both
        for c in range(0, nb, TILE):
            block = inverses[m, c : c + TILE, c : c + TILE]
            extra = jnp.where(eye, diag[m][:, c : c + TILE], 0.0)
            inverses[m, c : c + TILE, c : c + TILE] = block + extra
    sweep_inverse(inverses, tiles, columns, rows, 64, True)
    store = pltpu.make_async_copy(inverses, inverses_hbm, sems.at[2])
    store.start()
    own_state = [state[s : s + 1, :] for s in range(3)]
    arrived = incoming[...]
    given = message[:, nv + 3 * nb + nk :]
    early_state = jnp.where(three, own_state[0], jnp.where(two, arrived, given))
    early_state = jnp.where(second, early_state, arrived)
    late_state = jnp.where(three, own_state[1], jnp.where(two, own_state[0], arrived))
    late_state = jnp.where(second, late_state, own_state[0])
    active = early_late(link_mask, nv + 3 * nb)
    linked = jnp.concatenate(
        [active[0] * early_state, active[1] * late_state, jnp.zeros((6, nk), F32)], axis=0
    )
    links = dot3_nt(linked, link_in[...])
    rhs = early_late(block_rhs, nv + 2 * nb)
    available = early_late(availability, nv + nb)
    total = jnp.zeros((1, nb), F32)
    for m in range(HOURS):
        avail[m : m + 1, :] = available[m]
        corrected = as_column(rhs[m] + links[m : m + 1, :])
        y = jnp.sum(corrected * inverses[m], axis=0, keepdims=True)
        solved[m : m + 1, :] = y
        total = total + available[m] * y
    middle = jnp.zeros((nb, nb), F32)
    for m in range(HOURS):
        middle = middle + inverses[m] * as_column(available[m]) * available[m]
    for load in loads:
        load.wait()
    gradient = jnp.sum(as_column(total) * border[...], axis=0, keepdims=True)
    coupled[...] = dot3_nt(middle, border_t[...])
    row = 0
    for i in range(0, nb, TILE):
        part = dot3(border_t[i : i + TILE, :], coupled[:, : i + TILE])
        for j in range(0, i + TILE, TILE):
            packed[row : row + TILE, :] = part[:, j : j + TILE]
            row += TILE
    packed[row:, :] = jnp.zeros((packed.shape[0] - row, TILE), F32)
    for t in range(nb // TILE):
        packed[row + t : row + t + 1, :] = gradient[:, t * TILE : (t + 1) * TILE]
    store.wait()


def finish_kernel(
    place, packed, first_diag, first_rhs, avail, solved, border_hbm, inverses_hbm,
    first_step, steps, sent,
    schur, border, inverses, columns, rows, sems, *tiles,
):
    nb = schur.shape[1]
    loads = [
        pltpu.make_async_copy(border_hbm, border, sems.at[0]),
        pltpu.make_async_copy(inverses_hbm, inverses, sems.at[1]),
    ]
    for load in loads:
        load.start()
    eye = diagonal()
    row = 0
    for i in range(0, nb, TILE):
        for j in range(0, i + TILE, TILE):
            block = packed[row : row + TILE, :]
            row += TILE
            if i == j:
                block = block + jnp.where(eye, first_diag[:, i : i + TILE], 0.0)
            else:
                schur[0, j : j + TILE, i : i + TILE] = block.T
            schur[0, i : i + TILE, j : j + TILE] = block
    sweep_inverse(schur, tiles, columns, rows, TILE, False)
    gradient = jnp.concatenate(
        [packed[row + t : row + t + 1, :] for t in range(nb // TILE)], axis=1
    )
    rhs = as_column(gradient - first_rhs[...])
    x = jnp.sum(rhs * schur[0], axis=0, keepdims=True)
    first_step[...] = x
    for load in loads:
        load.wait()
    v = jnp.sum(border[...] * x, axis=1, keepdims=True)
    for m in range(HOURS):
        w = as_column(avail[m : m + 1, :]) * v
        steps[m : m + 1, :] = solved[m : m + 1, :] - jnp.sum(
            w * inverses[m], axis=0, keepdims=True
        )
    sent[...] = jnp.where(place[1] == 1, steps[0:1, :], steps[1:2, :])


PARAMS = pltpu.CompilerParams(vmem_limit_bytes=56 * 2**20)


def sweep_scratch(count, n):
    return [
        pltpu.VMEM((count, n, 3 * TILE), BF16),
        pltpu.VMEM((count, 3 * TILE, n), BF16),
        pltpu.SemaphoreType.DMA((3,)),
        *(pltpu.VMEM((TILE, TILE), F32) for _ in range(count)),
    ]


def spaces(count, scalar, remote):
    return [
        pl.BlockSpec(
            memory_space=pltpu.SMEM if k in scalar else pl.ANY if k in remote else pltpu.VMEM
        )
        for k in range(count)
    ]


def summed_over_all(array):
    rows, width = array.shape
    half = rows // 2
    core = lax.axis_index(CORE)
    chips = lax.axis_size(CHIPS)
    pair = [(0, 1), (1, 0)]
    kept = lax.dynamic_slice_in_dim(array, core * half, half, 0)
    sent = lax.dynamic_slice_in_dim(array, (1 - core) * half, half, 0)
    mine = kept + lax.ppermute(sent, CORE, pair)
    pieces = mine.reshape(chips, half // chips, width)
    piece = lax.all_to_all(pieces, CHIPS, 0, 0, tiled=True).sum(axis=0)
    spread = jnp.broadcast_to(piece[None], (chips, *piece.shape))
    mine = lax.all_to_all(spread, CHIPS, 0, 0, tiled=True).reshape(half, width)
    other = lax.ppermute(mine, CORE, pair)
    first = core == 0
    return jnp.concatenate([jnp.where(first, mine, other), jnp.where(first, other, mine)], axis=0)


def on_device(
    barrier_scale, regularizer, availability, block_rhs, primal, link_mask, counts,
    constraints, border, link_out, link_in, first_diag, first_rhs,
):
    nb, nv = constraints.shape
    count = counts[0]
    core = lax.axis_index(CORE)
    second = core == 1
    devices = lax.axis_size(GRP_BLK)
    pair = [(0, 1), (1, 0)]
    place = jnp.stack([count, core])
    state = lax.dot_general(
        primal, link_out, NT, precision=HIGHEST, preferred_element_type=F32
    )
    two, three = count >= 2, count == 3
    last = jnp.where(three, state[2:], jnp.where(two, state[1:2], state[:1]))
    incoming = lax.ppermute(last, GRP_BLK, [(d, d + 1) for d in range(devices - 1)])
    fields = (barrier_scale, regularizer, availability, block_rhs, link_mask.astype(F32))
    lent = [jnp.where(second, field[:1], field[2:]) for field in fields]
    message = lax.ppermute(jnp.concatenate([*lent, state[1:2]], axis=1), CORE, pair)
    packed_rows = (nb // TILE) * (nb // TILE + 1) // 2 * TILE + 8
    packed_rows = -(-packed_rows // (devices * 8)) * devices * 8
    square = pltpu.VMEM((nb, nb), F32)
    pairs = pltpu.VMEM((HOURS, nb, nb), F32)
    inverses, packed, solved, avail = pl.pallas_call(
        hours_kernel,
        out_shape=(
            jax.ShapeDtypeStruct((HOURS, nb, nb), F32),
            jax.ShapeDtypeStruct((packed_rows, TILE), F32),
            jax.ShapeDtypeStruct((HOURS, nb), F32),
            jax.ShapeDtypeStruct((HOURS, nb), F32),
        ),
        in_specs=spaces(13, (0,), (11, 12)),
        out_specs=spaces(4, (), (0,)),
        scratch_shapes=[
            pairs, square, square, pltpu.VMEM((nb, nv), BF16), square, *sweep_scratch(HOURS, nb)
        ],
        compiler_params=PARAMS,
        name="hours",
    )(
        place, barrier_scale, regularizer, availability, block_rhs, link_mask, state, incoming,
        message, link_in, constraints, border, border.T,
    )
    total = summed_over_all(packed)
    first_step, steps, sent = pl.pallas_call(
        finish_kernel,
        out_shape=(
            jax.ShapeDtypeStruct((1, nb), F32),
            jax.ShapeDtypeStruct((HOURS, nb), F32),
            jax.ShapeDtypeStruct((1, nb), F32),
        ),
        in_specs=spaces(8, (0,), (6, 7)),
        scratch_shapes=[pltpu.VMEM((1, nb, nb), F32), square, pairs, *sweep_scratch(1, nb)],
        compiler_params=PARAMS,
        name="finish",
    )(place, total, first_diag[None], first_rhs[None], avail, solved, border, inverses)
    returned = lax.ppermute(sent, CORE, pair)
    slot = jnp.arange(3, dtype=jnp.int32)[:, None]
    lead = jnp.where(second & three, returned, jnp.where(second & ~two, steps[1:], steps[:1]))
    middle = jnp.where(second & three, steps[:1], steps[1:])
    end = jnp.where(second, steps[1:], returned)
    chosen = jnp.where(slot == 0, lead, jnp.where(slot == 1, middle, end))
    return jnp.where(slot < count, chosen, 0.0), first_step[0]


def solution(mesh):
    split_mesh = Mesh(mesh.devices.reshape(mesh.shape["grp"], 4, 4, 2), GRP_BLK)
    whole = P(GRP_BLK, None)
    placed = (whole,) * 6 + (P(GRP_BLK),) + (P(),) * 6
    return jax.shard_map(
        on_device, mesh=split_mesh, in_specs=placed, out_specs=(whole, P()), check_vma=False
    )
```

```python
import functools

import jax
import jax.numpy as jnp
from jax import lax
from jax.experimental import pallas as pl
from jax.experimental.pallas import tpu as pltpu
from jax.sharding import Mesh
from jax.sharding import PartitionSpec as P

GRP_BLK = ("grp", "blk_0", "blk_1", "blk_2")
CHIPS = ("grp", "blk_0", "blk_1")
CORE = "blk_2"
HOURS = 2
TILE = 128
PANEL = 8
HIGHEST = lax.Precision.HIGHEST
CHUNK = 256
F32 = jnp.float32
BF16 = jnp.bfloat16
NT = (((1,), (1,)), ((), ()))


def lanes_of(x, k):
    return jnp.broadcast_to(x[:, k : k + 1], x.shape)


def row_of(x, j):
    return jnp.broadcast_to(x[j : j + 1, :], x.shape)


def invert_tiles(refs, reach, work=()):
    work = list(work)
    done = 0
    shape = (PANEL, TILE)
    lane = lax.broadcasted_iota(jnp.int32, shape, 1)
    sub = lax.broadcasted_iota(jnp.int32, shape, 0)
    panels = TILE // PANEL
    groups = reach // PANEL
    each = range(len(refs))
    for base in range(0, TILE, reach):
        parts = [
            [ref[base + PANEL * g : base + PANEL * (g + 1), :] for g in range(groups)]
            for ref in refs
        ]
        before = [ref[...] for ref in refs] if reach < TILE else None
        for t in range(groups):
            lo = base + PANEL * t
            inside = (lane >= lo) & (lane < lo + PANEL)
            eye = lane == sub + lo
            rows = [parts[m][t] for m in each]
            cols = [[lanes_of(rows[m], lo + j) for j in range(PANEL)] for m in each]
            rows = [jnp.where(inside, jnp.where(eye, 1.0, 0.0), rows[m]) for m in each]
            for j in range(PANEL):
                own = sub == j
                inverse = [1.0 / row_of(cols[m][j], j) for m in each]
                pivot = [row_of(rows[m], j) * inverse[m] for m in each]
                col = [cols[m][j] for m in each]
                for q in range(j + 1, PANEL):
                    for m in each:
                        c = row_of(cols[m][q], j) * inverse[m]
                        cols[m][q] = jnp.where(own, c, cols[m][q] - col[m] * c)
                rows = [jnp.where(own, pivot[m], rows[m] - col[m] * pivot[m]) for m in each]
            others = [(t + s) % groups for s in range(1, groups)]
            for m in each:
                spread = [row_of(rows[m], j) for j in range(PANEL)]
                acc = {i: jnp.where(inside, 0.0, parts[m][i]) for i in others}
                for i in others[:1]:
                    for j in range(PANEL):
                        acc[i] = acc[i] - lanes_of(parts[m][i], lo + j) * spread[j]
                for j in range(PANEL):
                    for i in others[1:]:
                        acc[i] = acc[i] - lanes_of(parts[m][i], lo + j) * spread[j]
                for i in others:
                    parts[m][i] = acc[i]
                parts[m][t] = rows[m]
            past = lo // PANEL + 1
            while done < len(work) and done * panels < past * len(work):
                work[done]()
                done += 1
        if reach == TILE:
            for m in each:
                for g in range(groups):
                    refs[m][PANEL * g : PANEL * (g + 1), :] = parts[m][g]
            continue
        wide = lax.broadcasted_iota(jnp.int32, (TILE, TILE), 1)
        tall = lax.broadcasted_iota(jnp.int32, (TILE, TILE), 0)
        own_lanes = (wide >= base) & (wide < base + reach)
        own_rows = (tall >= base) & (tall < base + reach)
        for m in each:
            block = list(parts[m])
            if base:
                block.insert(0, jnp.zeros((base, TILE), F32))
            if base + reach < TILE:
                block.append(jnp.zeros((TILE - base - reach, TILE), F32))
            block = jnp.concatenate(block, axis=0)
            bh, bl = split(block)
            xh, xl = split(before[m])
            change = mm(jnp.concatenate([xh, xl], 1), jnp.concatenate([bh, bh], 0)) + mm(xh, bl)
            rest = jnp.where(own_lanes, 0.0, before[m]) - change
            refs[m][...] = jnp.where(own_rows, block, rest)


def mm(a, b):
    return jnp.dot(a, b, preferred_element_type=F32)


def split(x):
    hi = x.astype(BF16)
    return hi, (x - hi.astype(F32)).astype(BF16)


def left(x):
    h, l = split(x)
    return jnp.concatenate([h, h, l], 1)


def right(x):
    h, l = split(x)
    return jnp.concatenate([h, l, h], 0)


def dot3(a, b):
    return mm(left(a), right(b))


def dot3_nt(a, b):
    h, l = split(b)
    return lax.dot_general(
        left(a), jnp.concatenate([h, l, h], 1), NT, preferred_element_type=F32
    )


def sweep_inverse(mats, tiles, columns, rows, reach):
    count, n, _ = mats.shape
    each = range(count)
    last = n // TILE - 1

    def begin(k):
        at = pl.multiple_of(k * TILE, TILE)
        here = pl.ds(at, TILE)
        row = lax.broadcasted_iota(jnp.int32, (n, TILE), 0)
        pivot_rows = (row >= at) & (row < at + TILE)
        for m in each:
            inverse = tiles[m][...]
            scaled = dot3(inverse, mats[m, here, :])
            columns[m] = left(jnp.where(pivot_rows, 0.0, mats[m, :, here]))
            mats[m, :, here] = jnp.zeros((n, TILE), F32)
            mats[m, here, :] = scaled
            mats[m, here, here] = inverse
            rows[m] = right(mats[m, here, :])

    def update(m, c):
        at = slice(c, c + CHUNK)
        mats[m, :, at] = mats[m, :, at] - mm(columns[m], rows[m, :, at])

    work = [functools.partial(update, m, c) for c in range(0, n, CHUNK) for m in each]

    def step(k, carry):
        begin(k)
        after = pl.ds(pl.multiple_of((k + 1) * TILE, TILE), TILE)
        for m in each:
            tiles[m][...] = mats[m, after, after] - mm(columns[m, after, :], rows[m, :, after])
        invert_tiles([tiles[m] for m in each], reach, work)
        return carry

    for m in each:
        tiles[m][...] = mats[m, :TILE, :TILE]
    invert_tiles([tiles[m] for m in each], reach)
    lax.fori_loop(0, last, step, 0)
    begin(last)
    for item in work:
        item()


def as_column(row):
    n = row.shape[1]
    eye = lax.broadcasted_iota(jnp.int32, (TILE, TILE), 0) == lax.broadcasted_iota(
        jnp.int32, (TILE, TILE), 1
    )
    parts = []
    for t in range(0, n, TILE):
        wide = jnp.broadcast_to(row[:, t : t + TILE], (TILE, TILE))
        parts.append(jnp.sum(jnp.where(eye, wide, 0.0), axis=1, keepdims=True))
    return jnp.concatenate(parts, axis=0)


def diagonal():
    return lax.broadcasted_iota(jnp.int32, (TILE, TILE), 0) == lax.broadcasted_iota(
        jnp.int32, (TILE, TILE), 1
    )


def hours_kernel(
    place, barrier_scale, regularizer, availability, block_rhs, link_mask, state, incoming, message,
    link_in, constraints, border_hbm, border_t_hbm,
    inverses_hbm, kept, lent, solved, avail,
    inverses, border, border_t, scaled, coupled, columns, rows, sems, *tiles,
):
    nb, nv = constraints.shape
    nk = link_in.shape[1]
    loads = [
        pltpu.make_async_copy(border_hbm, border, sems.at[0]),
        pltpu.make_async_copy(border_t_hbm, border_t, sems.at[1]),
    ]
    for load in loads:
        load.start()
    count, second = place[0], place[1] == 1
    two, three = count >= 2, count == 3
    eye = diagonal()

    def early_late(field, at):
        own = [field[s : s + 1, :].astype(F32) for s in range(3)]
        borrowed = message[:, at : at + field.shape[1]]
        early = jnp.where(two, jnp.where(second & three, own[1], own[0]), borrowed)
        early = jnp.where(second, early, own[0])
        late = jnp.where(three, own[2], jnp.where(two, own[1], own[0]))
        late = jnp.where(second, late, jnp.where(two, own[1], borrowed))
        return early, late

    scale = early_late(barrier_scale, 0)
    diag = early_late(regularizer, nv)
    for m in range(HOURS):
        scaled[...] = (constraints[...].astype(F32) * scale[m]).astype(BF16)
        for c in range(0, nb, CHUNK):
            inverses[m, :, c : c + CHUNK] = lax.dot_general(
                scaled[...], constraints[c : c + CHUNK, :], NT, preferred_element_type=F32
            )
        for i in range(0, nb, TILE):
            down = slice(i, i + TILE)
            for j in range(0, i, TILE):
                across = slice(j, j + TILE)
                block = 0.5 * (inverses[m, down, across] + inverses[m, across, down].T)
                inverses[m, down, across] = block
                inverses[m, across, down] = block.T
            block = inverses[m, down, down]
            extra = jnp.where(eye, diag[m][:, down], 0.0)
            inverses[m, down, down] = 0.5 * (block + block.T) + extra
    sweep_inverse(inverses, tiles, columns, rows, 64)
    store = pltpu.make_async_copy(inverses, inverses_hbm, sems.at[2])
    store.start()
    own_state = [state[s : s + 1, :] for s in range(3)]
    arrived = incoming[...]
    given = message[:, nv + 3 * nb + nk :]
    early_state = jnp.where(three, own_state[0], jnp.where(two, arrived, given))
    early_state = jnp.where(second, early_state, arrived)
    late_state = jnp.where(three, own_state[1], jnp.where(two, own_state[0], arrived))
    late_state = jnp.where(second, late_state, own_state[0])
    active = early_late(link_mask, nv + 3 * nb)
    linked = jnp.concatenate(
        [active[0] * early_state, active[1] * late_state, jnp.zeros((6, nk), F32)], axis=0
    )
    links = dot3_nt(linked, link_in[...])
    rhs = early_late(block_rhs, nv + 2 * nb)
    available = early_late(availability, nv + nb)
    total = jnp.zeros((1, nb), F32)
    for m in range(HOURS):
        avail[m : m + 1, :] = available[m]
        corrected = as_column(rhs[m] + links[m : m + 1, :])
        y = jnp.sum(corrected * inverses[m], axis=0, keepdims=True)
        solved[m : m + 1, :] = y
        total = total + available[m] * y
    middle = jnp.zeros((nb, nb), F32)
    for m in range(HOURS):
        middle = middle + inverses[m] * as_column(available[m]) * available[m]
    for load in loads:
        load.wait()
    gradient = jnp.sum(as_column(total) * border[...], axis=0, keepdims=True)
    coupled[...] = dot3_nt(middle, border_t[...])
    half = kept.shape[0]

    def put(row, value):
        first = (row < half) == (place[1] == 0)
        at = slice(row % half, row % half + value.shape[0])

        @pl.when(first)
        def _():
            kept[at, :] = value

        @pl.when(jnp.logical_not(first))
        def _():
            lent[at, :] = value

    row = 0
    for i in range(0, nb, TILE):
        part = dot3(border_t[i : i + TILE, :], coupled[:, : i + TILE])
        for j in range(0, i + TILE, TILE):
            put(row, part[:, j : j + TILE])
            row += TILE
    parts = [gradient[:, t * TILE : (t + 1) * TILE] for t in range(nb // TILE)]
    parts.append(jnp.zeros((2 * half - row - len(parts), TILE), F32))
    put(row, jnp.concatenate(parts, axis=0))
    store.wait()


def as_row(column):
    wide = jnp.broadcast_to(column, (TILE, TILE))
    return jnp.sum(jnp.where(diagonal(), wide, 0.0), axis=0, keepdims=True)


def finish_kernel(
    place, mine, other, first_diag, first_rhs, avail, solved, border_hbm, inverses_hbm,
    first_step, steps, sent,
    schur, rhs, heads, border, inverses, sems, tile,
):
    nb = schur.shape[0]
    count = nb // TILE
    half = mine.shape[0]
    loads = [
        pltpu.make_async_copy(border_hbm, border, sems.at[0]),
        pltpu.make_async_copy(inverses_hbm, inverses, sems.at[1]),
    ]
    for load in loads:
        load.start()
    eye = diagonal()

    def get(row, rows):
        at = slice(row % half, row % half + rows)
        return jnp.where((row < half) == (place[1] == 0), mine[at, :], other[at, :])

    row = 0
    for i in range(0, nb, TILE):
        for j in range(0, i + TILE, TILE):
            block = get(row, TILE)
            row += TILE
            if i == j:
                block = block + jnp.where(eye, first_diag[:, i : i + TILE], 0.0)
            schur[i : i + TILE, j : j + TILE] = block
    tail = get(row, 8)
    gradient = jnp.concatenate([tail[t : t + 1, :] for t in range(count)], axis=1)
    rhs[...] = as_column(gradient - first_rhs[...])

    def eliminate(k):
        here, below = slice(k * TILE, (k + 1) * TILE), slice((k + 1) * TILE, nb)
        pivot = tile[...]
        column = schur[below, here]
        scaled = dot3(column, pivot)
        factor = left(scaled)
        h, l = split(column)
        across = jnp.concatenate([h, l, h], 1)
        for c in range(0, nb - (k + 1) * TILE, TILE):
            start = (k + 1) * TILE + c
            at = (slice(start, nb), slice(start, start + TILE))
            schur[at] = schur[at] - lax.dot_general(
                factor[c:, :], across[c : c + TILE, :], NT, preferred_element_type=F32
            )
        schur[below, here] = scaled
        own = rhs[here, :]
        heads[k : k + 1, :] = jnp.sum(own * pivot, axis=0, keepdims=True)
        rhs[below, :] = rhs[below, :] - jnp.sum(scaled * as_row(own), axis=1, keepdims=True)

    def step(k, carry):
        for done in range(1, count):
            pl.when(k == done)(functools.partial(eliminate, done - 1))
        here = pl.ds(pl.multiple_of(k * TILE, TILE), TILE)
        tile[...] = schur[here, here]
        invert_tiles([tile], TILE)
        return carry

    lax.fori_loop(0, count, step, 0)
    x = jnp.sum(rhs[nb - TILE :, :] * tile[...], axis=0, keepdims=True)
    found_row, found_column = x, as_column(x)
    for k in range(count - 2, -1, -1):
        below = schur[(k + 1) * TILE :, k * TILE : (k + 1) * TILE]
        x = heads[k : k + 1, :] - jnp.sum(found_column * below, axis=0, keepdims=True)
        found_row = jnp.concatenate([x, found_row], axis=1)
        found_column = jnp.concatenate([as_column(x), found_column], axis=0)
    first_step[...] = found_row
    for load in loads:
        load.wait()
    v = jnp.sum(border[...] * found_row, axis=1, keepdims=True)
    for m in range(HOURS):
        w = as_column(avail[m : m + 1, :]) * v
        steps[m : m + 1, :] = solved[m : m + 1, :] - jnp.sum(
            w * inverses[m], axis=0, keepdims=True
        )
    sent[...] = jnp.where(place[1] == 1, steps[0:1, :], steps[1:2, :])


def message_kernel(
    place, barrier_scale, regularizer, availability, block_rhs, link_mask, primal, link_out,
    state, last, message,
):
    padded = jnp.concatenate([primal[...], jnp.zeros((5, primal.shape[1]), F32)], axis=0)
    states = dot3_nt(padded, link_out[...])
    state[...] = states[:3, :]
    count, second = place[0], place[1] == 1
    last[...] = jnp.where(
        count == 3, states[2:3, :], jnp.where(count == 2, states[1:2, :], states[:1, :])
    )
    at = 0
    for field in (barrier_scale, regularizer, availability, block_rhs, link_mask):
        width = field.shape[1]
        lent = jnp.where(second, field[0:1, :], field[2:3, :])
        message[:, at : at + width] = lent.astype(F32)
        at += width
    message[:, at:] = states[1:2, :]


PARAMS = pltpu.CompilerParams(vmem_limit_bytes=56 * 2**20)


def sweep_scratch(count, n):
    return [
        pltpu.VMEM((count, n, 3 * TILE), BF16),
        pltpu.VMEM((count, 3 * TILE, n), BF16),
        pltpu.SemaphoreType.DMA((3,)),
        *(pltpu.VMEM((TILE, TILE), F32) for _ in range(count)),
    ]


def spaces(count, scalar, remote):
    return [
        pl.BlockSpec(
            memory_space=pltpu.SMEM if k in scalar else pl.ANY if k in remote else pltpu.VMEM
        )
        for k in range(count)
    ]


def summed_over_chips(array):
    rows, width = array.shape
    chips = lax.axis_size(CHIPS)
    pieces = array.reshape(chips, rows // chips, width)
    piece = lax.all_to_all(pieces, CHIPS, 0, 0, tiled=True).sum(axis=0)
    spread = jnp.broadcast_to(piece[None], (chips, *piece.shape))
    return lax.all_to_all(spread, CHIPS, 0, 0, tiled=True).reshape(rows, width)


def on_device(
    barrier_scale, regularizer, availability, block_rhs, primal, link_mask, counts,
    constraints, border, link_out, link_in, first_diag, first_rhs,
):
    nb, nv = constraints.shape
    count = counts[0]
    core = lax.axis_index(CORE)
    second = core == 1
    devices = lax.axis_size(GRP_BLK)
    pair = [(0, 1), (1, 0)]
    place = jnp.stack([count, core])
    three, two = count == 3, count >= 2
    nk = link_in.shape[1]
    state, last, lent = pl.pallas_call(
        message_kernel,
        out_shape=(
            jax.ShapeDtypeStruct((3, nk), F32),
            jax.ShapeDtypeStruct((1, nk), F32),
            jax.ShapeDtypeStruct((1, nv + 3 * nb + 2 * nk), F32),
        ),
        in_specs=spaces(8, (0,), ()),
        compiler_params=PARAMS,
        name="message",
    )(place, barrier_scale, regularizer, availability, block_rhs, link_mask, primal, link_out)
    incoming = lax.ppermute(last, GRP_BLK, [(d, d + 1) for d in range(devices - 1)])
    message = lax.ppermute(lent, CORE, pair)
    packed_rows = (nb // TILE) * (nb // TILE + 1) // 2 * TILE + 8
    packed_rows = -(-packed_rows // (devices * 8)) * devices * 8
    square = pltpu.VMEM((nb, nb), F32)
    pairs = pltpu.VMEM((HOURS, nb, nb), F32)
    inverses, kept, sent, solved, avail = pl.pallas_call(
        hours_kernel,
        out_shape=(
            jax.ShapeDtypeStruct((HOURS, nb, nb), F32),
            jax.ShapeDtypeStruct((packed_rows // 2, TILE), F32),
            jax.ShapeDtypeStruct((packed_rows // 2, TILE), F32),
            jax.ShapeDtypeStruct((HOURS, nb), F32),
            jax.ShapeDtypeStruct((HOURS, nb), F32),
        ),
        in_specs=spaces(13, (0,), (11, 12)),
        out_specs=spaces(5, (), (0,)),
        scratch_shapes=[
            pairs, square, square, pltpu.VMEM((nb, nv), BF16), square, *sweep_scratch(HOURS, nb)
        ],
        compiler_params=PARAMS,
        name="hours",
    )(
        place, barrier_scale, regularizer, availability, block_rhs, link_mask, state, incoming,
        message, link_in, constraints, border, border.T,
    )
    mine = summed_over_chips(kept + lax.ppermute(sent, CORE, pair))
    other = lax.ppermute(mine, CORE, pair)
    first_step, steps, sent = pl.pallas_call(
        finish_kernel,
        out_shape=(
            jax.ShapeDtypeStruct((1, nb), F32),
            jax.ShapeDtypeStruct((HOURS, nb), F32),
            jax.ShapeDtypeStruct((1, nb), F32),
        ),
        in_specs=spaces(9, (0,), (7, 8)),
        scratch_shapes=[
            square, pltpu.VMEM((nb, 1), F32), pltpu.VMEM((8, TILE), F32), square, pairs,
            pltpu.SemaphoreType.DMA((2,)), pltpu.VMEM((TILE, TILE), F32),
        ],
        compiler_params=PARAMS,
        name="finish",
    )(place, mine, other, first_diag[None], first_rhs[None], avail, solved, border, inverses)
    returned = lax.ppermute(sent, CORE, pair)
    slot = jnp.arange(3, dtype=jnp.int32)[:, None]
    lead = jnp.where(second & three, returned, jnp.where(second & ~two, steps[1:], steps[:1]))
    middle = jnp.where(second & three, steps[:1], steps[1:])
    end = jnp.where(second, steps[1:], returned)
    chosen = jnp.where(slot == 0, lead, jnp.where(slot == 1, middle, end))
    return jnp.where(slot < count, chosen, 0.0), first_step[0]


def solution(mesh):
    split_mesh = Mesh(mesh.devices.reshape(mesh.shape["grp"], 4, 4, 2), GRP_BLK)
    whole = P(GRP_BLK, None)
    placed = (whole,) * 6 + (P(GRP_BLK),) + (P(),) * 6
    return jax.shard_map(
        on_device, mesh=split_mesh, in_specs=placed, out_specs=(whole, P()), check_vma=False
    )
```

```python
import functools

import jax
import jax.numpy as jnp
from jax import lax
from jax.experimental import pallas as pl
from jax.experimental.pallas import tpu as pltpu
from jax.sharding import Mesh
from jax.sharding import PartitionSpec as P

GRP_BLK = ("grp", "blk_0", "blk_1", "blk_2")
CHIPS = ("grp", "blk_0", "blk_1")
CORE = "blk_2"
HOURS = 2
TILE = 128
PANEL = 8
HIGHEST = lax.Precision.HIGHEST
CHUNK = 256
F32 = jnp.float32
BF16 = jnp.bfloat16
NT = (((1,), (1,)), ((), ()))


def lanes_of(x, k):
    return jnp.broadcast_to(x[:, k : k + 1], x.shape)


def row_of(x, j):
    return jnp.broadcast_to(x[j : j + 1, :], x.shape)


def invert_tiles(refs, window, work=()):
    work = list(work)
    done = 0
    shape = (PANEL, TILE)
    lane = lax.broadcasted_iota(jnp.int32, shape, 1)
    sub = lax.broadcasted_iota(jnp.int32, shape, 0)
    panels = TILE // PANEL
    groups = window // PANEL
    windows = TILE // window
    each = range(len(refs))
    parts = [[ref[PANEL * g : PANEL * (g + 1), :] for g in range(panels)] for ref in refs]
    for w in range(windows):
        near = range(groups * w, min(groups * (w + 2), panels))
        for t in range(groups * w, groups * (w + 1)):
            lo = PANEL * t
            inside = (lane >= lo) & (lane < lo + PANEL)
            eye = lane == sub + lo
            rows = [parts[m][t] for m in each]
            cols = [[lanes_of(rows[m], lo + j) for j in range(PANEL)] for m in each]
            rows = [jnp.where(inside, jnp.where(eye, 1.0, 0.0), rows[m]) for m in each]
            for j in range(PANEL):
                own = sub == j
                inverse = [1.0 / row_of(cols[m][j], j) for m in each]
                pivot = [row_of(rows[m], j) * inverse[m] for m in each]
                col = [cols[m][j] for m in each]
                for q in range(j + 1, PANEL):
                    for m in each:
                        c = row_of(cols[m][q], j) * inverse[m]
                        cols[m][q] = jnp.where(own, c, cols[m][q] - col[m] * c)
                rows = [jnp.where(own, pivot[m], rows[m] - col[m] * pivot[m]) for m in each]
            others = [i for i in near if i > t] + [i for i in near if i < t]
            for m in each:
                spread = [row_of(rows[m], j) for j in range(PANEL)]
                acc = {i: jnp.where(inside, 0.0, parts[m][i]) for i in others}
                for i in others[:1]:
                    for j in range(PANEL):
                        acc[i] = acc[i] - lanes_of(parts[m][i], lo + j) * spread[j]
                for j in range(PANEL):
                    for i in others[1:]:
                        acc[i] = acc[i] - lanes_of(parts[m][i], lo + j) * spread[j]
                for i in others:
                    parts[m][i] = acc[i]
                parts[m][t] = rows[m]
            past = t + 1
            while done < len(work) and done * panels < past * len(work):
                work[done]()
                done += 1
        far = [i for i in range(panels) if i not in near]
        if not far:
            continue
        base = window * w
        wide = lax.broadcasted_iota(jnp.int32, (PANEL * len(far), TILE), 1)
        own_lanes = (wide >= base) & (wide < base + window)
        for m in each:
            block = parts[m][groups * w : groups * (w + 1)]
            above, under = base, TILE - base - window
            if above:
                block = [jnp.zeros((above, TILE), F32), *block]
            if under:
                block = [*block, jnp.zeros((under, TILE), F32)]
            bh, bl = split(jnp.concatenate(block, axis=0))
            old = jnp.concatenate([parts[m][i] for i in far], axis=0)
            xh, xl = split(old)
            change = mm(jnp.concatenate([xh, xl], 1), jnp.concatenate([bh, bh], 0)) + mm(xh, bl)
            new = jnp.where(own_lanes, 0.0, old) - change
            for s, i in enumerate(far):
                parts[m][i] = new[PANEL * s : PANEL * (s + 1), :]
    for m in each:
        for g in range(panels):
            refs[m][PANEL * g : PANEL * (g + 1), :] = parts[m][g]


def mm(a, b):
    return jnp.dot(a, b, preferred_element_type=F32)


def split(x):
    hi = x.astype(BF16)
    return hi, (x - hi.astype(F32)).astype(BF16)


def left(x):
    h, l = split(x)
    return jnp.concatenate([h, h, l], 1)


def right(x):
    h, l = split(x)
    return jnp.concatenate([h, l, h], 0)


def dot3(a, b):
    return mm(left(a), right(b))


def dot3_nt(a, b):
    h, l = split(b)
    return lax.dot_general(
        left(a), jnp.concatenate([h, l, h], 1), NT, preferred_element_type=F32
    )


def sweep_inverse(mats, tiles, columns, rows, window):
    count, n, _ = mats.shape
    each = range(count)
    tiles, saved = tiles[:count], tiles[count:]
    last = n // TILE - 1

    def begin(k, m):
        at = pl.multiple_of(k * TILE, TILE)
        here = pl.ds(at, TILE)
        row = lax.broadcasted_iota(jnp.int32, (n, TILE), 0)
        pivot_rows = (row >= at) & (row < at + TILE)
        inverse = saved[m][...]
        scaled = dot3(inverse, mats[m, here, :])
        columns[m] = left(jnp.where(pivot_rows, 0.0, mats[m, :, here]))
        mats[m, :, here] = jnp.zeros((n, TILE), F32)
        mats[m, here, :] = scaled
        mats[m, here, here] = inverse
        rows[m] = right(mats[m, here, :])

    def update(m, c):
        at = slice(c, c + CHUNK)
        mats[m, :, at] = mats[m, :, at] - mm(columns[m], rows[m, :, at])

    work = [functools.partial(update, m, c) for c in range(0, n, CHUNK) for m in each]

    def step(k, carry):
        here = pl.ds(pl.multiple_of(k * TILE, TILE), TILE)
        after = pl.ds(pl.multiple_of((k + 1) * TILE, TILE), TILE)
        for m in each:
            inverse = tiles[m][...]
            saved[m][...] = inverse
            scaled = dot3(inverse, mats[m, here, after])
            tiles[m][...] = mats[m, after, after] - dot3(mats[m, after, here], scaled)
        begins = [functools.partial(begin, k, m) for m in each]
        invert_tiles([tiles[m] for m in each], window, begins + work)
        return carry

    for m in each:
        tiles[m][...] = mats[m, :TILE, :TILE]
    invert_tiles([tiles[m] for m in each], window)
    lax.fori_loop(0, last, step, 0)
    for m in each:
        saved[m][...] = tiles[m][...]
        begin(last, m)
    for item in work:
        item()


def as_column(row):
    n = row.shape[1]
    eye = lax.broadcasted_iota(jnp.int32, (TILE, TILE), 0) == lax.broadcasted_iota(
        jnp.int32, (TILE, TILE), 1
    )
    parts = []
    for t in range(0, n, TILE):
        wide = jnp.broadcast_to(row[:, t : t + TILE], (TILE, TILE))
        parts.append(jnp.sum(jnp.where(eye, wide, 0.0), axis=1, keepdims=True))
    return jnp.concatenate(parts, axis=0)


def diagonal():
    return lax.broadcasted_iota(jnp.int32, (TILE, TILE), 0) == lax.broadcasted_iota(
        jnp.int32, (TILE, TILE), 1
    )


def hours_kernel(
    place, barrier_scale, regularizer, availability, block_rhs, link_mask, state, incoming, message,
    link_in, constraints, border_hbm, border_t_hbm,
    inverses_hbm, kept, lent, solved, avail,
    inverses, border, border_t, scaled, coupled, columns, rows, sems, *tiles,
):
    nb, nv = constraints.shape
    nk = link_in.shape[1]
    loads = [
        pltpu.make_async_copy(border_hbm, border, sems.at[0]),
        pltpu.make_async_copy(border_t_hbm, border_t, sems.at[1]),
    ]
    for load in loads:
        load.start()
    count, second = place[0], place[1] == 1
    two, three = count >= 2, count == 3
    eye = diagonal()

    def early_late(field, at):
        own = [field[s : s + 1, :].astype(F32) for s in range(3)]
        borrowed = message[:, at : at + field.shape[1]]
        early = jnp.where(two, jnp.where(second & three, own[1], own[0]), borrowed)
        early = jnp.where(second, early, own[0])
        late = jnp.where(three, own[2], jnp.where(two, own[1], own[0]))
        late = jnp.where(second, late, jnp.where(two, own[1], borrowed))
        return early, late

    scale = early_late(barrier_scale, 0)
    diag = early_late(regularizer, nv)
    for m in range(HOURS):
        scaled[...] = (constraints[...].astype(F32) * scale[m]).astype(BF16)
        for c in range(0, nb, CHUNK):
            inverses[m, :, c : c + CHUNK] = lax.dot_general(
                scaled[...], constraints[c : c + CHUNK, :], NT, preferred_element_type=F32
            )
        for i in range(0, nb, TILE):
            down = slice(i, i + TILE)
            for j in range(0, i, TILE):
                across = slice(j, j + TILE)
                block = 0.5 * (inverses[m, down, across] + inverses[m, across, down].T)
                inverses[m, down, across] = block
                inverses[m, across, down] = block.T
            block = inverses[m, down, down]
            extra = jnp.where(eye, diag[m][:, down], 0.0)
            inverses[m, down, down] = 0.5 * (block + block.T) + extra
    sweep_inverse(inverses, tiles, columns, rows, 32)
    store = pltpu.make_async_copy(inverses, inverses_hbm, sems.at[2])
    store.start()
    own_state = [state[s : s + 1, :] for s in range(3)]
    arrived = incoming[...]
    given = message[:, nv + 3 * nb + nk :]
    early_state = jnp.where(three, own_state[0], jnp.where(two, arrived, given))
    early_state = jnp.where(second, early_state, arrived)
    late_state = jnp.where(three, own_state[1], jnp.where(two, own_state[0], arrived))
    late_state = jnp.where(second, late_state, own_state[0])
    active = early_late(link_mask, nv + 3 * nb)
    linked = jnp.concatenate(
        [active[0] * early_state, active[1] * late_state, jnp.zeros((6, nk), F32)], axis=0
    )
    links = dot3_nt(linked, link_in[...])
    rhs = early_late(block_rhs, nv + 2 * nb)
    available = early_late(availability, nv + nb)
    total = jnp.zeros((1, nb), F32)
    for m in range(HOURS):
        avail[m : m + 1, :] = available[m]
        corrected = as_column(rhs[m] + links[m : m + 1, :])
        y = jnp.sum(corrected * inverses[m], axis=0, keepdims=True)
        solved[m : m + 1, :] = y
        total = total + available[m] * y
    middle = jnp.zeros((nb, nb), F32)
    for m in range(HOURS):
        middle = middle + inverses[m] * as_column(available[m]) * available[m]
    for load in loads:
        load.wait()
    gradient = jnp.sum(as_column(total) * border[...], axis=0, keepdims=True)
    coupled[...] = dot3_nt(middle, border_t[...])
    half = kept.shape[0]

    def put(row, value):
        first = (row < half) == (place[1] == 0)
        at = slice(row % half, row % half + value.shape[0])

        @pl.when(first)
        def _():
            kept[at, :] = value

        @pl.when(jnp.logical_not(first))
        def _():
            lent[at, :] = value

    row = 0
    for i in range(0, nb, TILE):
        part = dot3(border_t[i : i + TILE, :], coupled[:, : i + TILE])
        for j in range(0, i + TILE, TILE):
            put(row, part[:, j : j + TILE])
            row += TILE
    parts = [gradient[:, t * TILE : (t + 1) * TILE] for t in range(nb // TILE)]
    parts.append(jnp.zeros((2 * half - row - len(parts), TILE), F32))
    put(row, jnp.concatenate(parts, axis=0))
    store.wait()


def as_row(column):
    wide = jnp.broadcast_to(column, (TILE, TILE))
    return jnp.sum(jnp.where(diagonal(), wide, 0.0), axis=0, keepdims=True)


def finish_kernel(
    place, mine, other, first_diag, first_rhs, avail, solved, border_hbm, inverses_hbm,
    first_step, steps, sent,
    schur, rhs, heads, border, inverses, sems, tile,
):
    nb = schur.shape[0]
    count = nb // TILE
    half = mine.shape[0]
    loads = [
        pltpu.make_async_copy(border_hbm, border, sems.at[0]),
        pltpu.make_async_copy(inverses_hbm, inverses, sems.at[1]),
    ]
    for load in loads:
        load.start()
    eye = diagonal()

    def get(row, rows):
        at = slice(row % half, row % half + rows)
        return jnp.where((row < half) == (place[1] == 0), mine[at, :], other[at, :])

    row = 0
    for i in range(0, nb, TILE):
        for j in range(0, i + TILE, TILE):
            block = get(row, TILE)
            row += TILE
            if i == j:
                block = block + jnp.where(eye, first_diag[i : i + TILE].reshape(1, TILE), 0.0)
            schur[i : i + TILE, j : j + TILE] = block
    tail = get(row, 8)
    gradient = jnp.concatenate([tail[t : t + 1, :] for t in range(count)], axis=1)
    rhs[...] = as_column(gradient - first_rhs[...].reshape(1, nb))

    def eliminate(k):
        here, below = slice(k * TILE, (k + 1) * TILE), slice((k + 1) * TILE, nb)
        pivot = tile[...]
        column = schur[below, here]
        scaled = dot3(column, pivot)
        factor = left(scaled)
        h, l = split(column)
        across = jnp.concatenate([h, l, h], 1)
        for c in range(0, nb - (k + 1) * TILE, TILE):
            start = (k + 1) * TILE + c
            at = (slice(start, nb), slice(start, start + TILE))
            schur[at] = schur[at] - lax.dot_general(
                factor[c:, :], across[c : c + TILE, :], NT, preferred_element_type=F32
            )
        schur[below, here] = scaled
        own = rhs[here, :]
        heads[k : k + 1, :] = jnp.sum(own * pivot, axis=0, keepdims=True)
        rhs[below, :] = rhs[below, :] - jnp.sum(scaled * as_row(own), axis=1, keepdims=True)

    def step(k, carry):
        for done in range(1, count):
            pl.when(k == done)(functools.partial(eliminate, done - 1))
        here = pl.ds(pl.multiple_of(k * TILE, TILE), TILE)
        tile[...] = schur[here, here]
        invert_tiles([tile], TILE // 2)
        return carry

    lax.fori_loop(0, count, step, 0)
    x = jnp.sum(rhs[nb - TILE :, :] * tile[...], axis=0, keepdims=True)
    found_row, found_column = x, as_column(x)
    for k in range(count - 2, -1, -1):
        below = schur[(k + 1) * TILE :, k * TILE : (k + 1) * TILE]
        x = heads[k : k + 1, :] - jnp.sum(found_column * below, axis=0, keepdims=True)
        found_row = jnp.concatenate([x, found_row], axis=1)
        found_column = jnp.concatenate([as_column(x), found_column], axis=0)
    first_step[...] = found_row.reshape(nb)
    for load in loads:
        load.wait()
    v = jnp.sum(border[...] * found_row, axis=1, keepdims=True)
    for m in range(HOURS):
        w = as_column(avail[m : m + 1, :]) * v
        steps[m : m + 1, :] = solved[m : m + 1, :] - jnp.sum(
            w * inverses[m], axis=0, keepdims=True
        )
    sent[...] = jnp.where(place[1] == 1, steps[0:1, :], steps[1:2, :])


def message_kernel(
    place, barrier_scale, regularizer, availability, block_rhs, link_mask, primal, link_out,
    state, last, message,
):
    padded = jnp.concatenate([primal[...], jnp.zeros((5, primal.shape[1]), F32)], axis=0)
    states = dot3_nt(padded, link_out[...])
    state[...] = states[:3, :]
    count, second = place[0], place[1] == 1
    last[...] = jnp.where(
        count == 3, states[2:3, :], jnp.where(count == 2, states[1:2, :], states[:1, :])
    )
    at = 0
    for field in (barrier_scale, regularizer, availability, block_rhs, link_mask):
        width = field.shape[1]
        lent = jnp.where(second, field[0:1, :], field[2:3, :])
        message[:, at : at + width] = lent.astype(F32)
        at += width
    message[:, at:] = states[1:2, :]


PARAMS = pltpu.CompilerParams(vmem_limit_bytes=56 * 2**20)


def sweep_scratch(count, n):
    return [
        pltpu.VMEM((count, n, 3 * TILE), BF16),
        pltpu.VMEM((count, 3 * TILE, n), BF16),
        pltpu.SemaphoreType.DMA((3,)),
        *(pltpu.VMEM((TILE, TILE), F32) for _ in range(2 * count)),
    ]


def spaces(count, scalar, remote):
    return [
        pl.BlockSpec(
            memory_space=pltpu.SMEM if k in scalar else pl.ANY if k in remote else pltpu.VMEM
        )
        for k in range(count)
    ]


def summed_over_chips(array):
    rows, width = array.shape
    chips = lax.axis_size(CHIPS)
    pieces = array.reshape(chips, rows // chips, width)
    piece = lax.all_to_all(pieces, CHIPS, 0, 0, tiled=True).sum(axis=0)
    spread = jnp.broadcast_to(piece[None], (chips, *piece.shape))
    return lax.all_to_all(spread, CHIPS, 0, 0, tiled=True).reshape(rows, width)


def on_device(
    barrier_scale, regularizer, availability, block_rhs, primal, link_mask, counts,
    constraints, border, link_out, link_in, first_diag, first_rhs,
):
    nb, nv = constraints.shape
    count = counts[0]
    core = lax.axis_index(CORE)
    second = core == 1
    devices = lax.axis_size(GRP_BLK)
    pair = [(0, 1), (1, 0)]
    place = jnp.stack([count, core])
    three, two = count == 3, count >= 2
    nk = link_in.shape[1]
    state, last, lent = pl.pallas_call(
        message_kernel,
        out_shape=(
            jax.ShapeDtypeStruct((3, nk), F32),
            jax.ShapeDtypeStruct((1, nk), F32),
            jax.ShapeDtypeStruct((1, nv + 3 * nb + 2 * nk), F32),
        ),
        in_specs=spaces(8, (0,), ()),
        compiler_params=PARAMS,
        name="message",
    )(place, barrier_scale, regularizer, availability, block_rhs, link_mask, primal, link_out)
    incoming = lax.ppermute(last, GRP_BLK, [(d, d + 1) for d in range(devices - 1)])
    message = lax.ppermute(lent, CORE, pair)
    packed_rows = (nb // TILE) * (nb // TILE + 1) // 2 * TILE + 8
    packed_rows = -(-packed_rows // (devices * 8)) * devices * 8
    square = pltpu.VMEM((nb, nb), F32)
    pairs = pltpu.VMEM((HOURS, nb, nb), F32)
    inverses, kept, sent, solved, avail = pl.pallas_call(
        hours_kernel,
        out_shape=(
            jax.ShapeDtypeStruct((HOURS, nb, nb), F32),
            jax.ShapeDtypeStruct((packed_rows // 2, TILE), F32),
            jax.ShapeDtypeStruct((packed_rows // 2, TILE), F32),
            jax.ShapeDtypeStruct((HOURS, nb), F32),
            jax.ShapeDtypeStruct((HOURS, nb), F32),
        ),
        in_specs=spaces(13, (0,), (11, 12)),
        out_specs=spaces(5, (), (0,)),
        scratch_shapes=[
            pairs, square, square, pltpu.VMEM((nb, nv), BF16), square, *sweep_scratch(HOURS, nb)
        ],
        compiler_params=PARAMS,
        name="hours",
    )(
        place, barrier_scale, regularizer, availability, block_rhs, link_mask, state, incoming,
        message, link_in, constraints, border, border.T,
    )
    mine = summed_over_chips(kept + lax.ppermute(sent, CORE, pair))
    other = lax.ppermute(mine, CORE, pair)
    first_step, steps, sent = pl.pallas_call(
        finish_kernel,
        out_shape=(
            jax.ShapeDtypeStruct((nb,), F32),
            jax.ShapeDtypeStruct((HOURS, nb), F32),
            jax.ShapeDtypeStruct((1, nb), F32),
        ),
        in_specs=spaces(9, (0,), (7, 8)),
        scratch_shapes=[
            square, pltpu.VMEM((nb, 1), F32), pltpu.VMEM((8, TILE), F32), square, pairs,
            pltpu.SemaphoreType.DMA((2,)), pltpu.VMEM((TILE, TILE), F32),
        ],
        compiler_params=PARAMS,
        name="finish",
    )(place, mine, other, first_diag, first_rhs, avail, solved, border, inverses)
    returned = lax.ppermute(sent, CORE, pair)
    slot = jnp.arange(3, dtype=jnp.int32)[:, None]
    lead = jnp.where(second & three, returned, jnp.where(second & ~two, steps[1:], steps[:1]))
    middle = jnp.where(second & three, steps[:1], steps[1:])
    end = jnp.where(second, steps[1:], returned)
    chosen = jnp.where(slot == 0, lead, jnp.where(slot == 1, middle, end))
    return jnp.where(slot < count, chosen, 0.0), first_step


def solution(mesh):
    split_mesh = Mesh(mesh.devices.reshape(mesh.shape["grp"], 4, 4, 2), GRP_BLK)
    whole = P(GRP_BLK, None)
    placed = (whole,) * 6 + (P(GRP_BLK),) + (P(),) * 6
    return jax.shard_map(
        on_device, mesh=split_mesh, in_specs=placed, out_specs=(whole, P()), check_vma=False
    )
```

```python
import functools

import jax
import jax.numpy as jnp
from jax import lax
from jax.experimental import pallas as pl
from jax.experimental.pallas import tpu as pltpu
from jax.sharding import Mesh
from jax.sharding import PartitionSpec as P

GRP_BLK = ("grp", "blk_0", "blk_1", "blk_2")
CHIPS = ("grp", "blk_0", "blk_1")
CORE = "blk_2"
HOURS = 2
TILE = 128
PANEL = 8
HIGHEST = lax.Precision.HIGHEST
CHUNK = 256
F32 = jnp.float32
BF16 = jnp.bfloat16
NT = (((1,), (1,)), ((), ()))


def lanes_of(x, k):
    return jnp.broadcast_to(x[:, k : k + 1], x.shape)


def row_of(x, j):
    return jnp.broadcast_to(x[j : j + 1, :], x.shape)


def invert_tiles(refs, window, work=()):
    work = list(work)
    done = 0
    shape = (PANEL, TILE)
    lane = lax.broadcasted_iota(jnp.int32, shape, 1)
    sub = lax.broadcasted_iota(jnp.int32, shape, 0)
    panels = TILE // PANEL
    groups = window // PANEL
    windows = TILE // window
    each = range(len(refs))
    parts = [[ref[PANEL * g : PANEL * (g + 1), :] for g in range(panels)] for ref in refs]
    for w in range(windows):
        near = range(groups * w, min(groups * (w + 2), panels))
        for t in range(groups * w, groups * (w + 1)):
            lo = PANEL * t
            inside = (lane >= lo) & (lane < lo + PANEL)
            eye = lane == sub + lo
            rows = [parts[m][t] for m in each]
            cols = [[lanes_of(rows[m], lo + j) for j in range(PANEL)] for m in each]
            rows = [jnp.where(inside, jnp.where(eye, 1.0, 0.0), rows[m]) for m in each]
            for j in range(PANEL):
                own = sub == j
                inverse = [1.0 / row_of(cols[m][j], j) for m in each]
                pivot = [row_of(rows[m], j) * inverse[m] for m in each]
                col = [cols[m][j] for m in each]
                for q in range(j + 1, PANEL):
                    for m in each:
                        c = row_of(cols[m][q], j) * inverse[m]
                        cols[m][q] = jnp.where(own, c, cols[m][q] - col[m] * c)
                rows = [jnp.where(own, pivot[m], rows[m] - col[m] * pivot[m]) for m in each]
            others = [i for i in near if i > t] + [i for i in near if i < t]
            for m in each:
                spread = [row_of(rows[m], j) for j in range(PANEL)]
                acc = {i: jnp.where(inside, 0.0, parts[m][i]) for i in others}
                for i in others[:1]:
                    for j in range(PANEL):
                        acc[i] = acc[i] - lanes_of(parts[m][i], lo + j) * spread[j]
                for j in range(PANEL):
                    for i in others[1:]:
                        acc[i] = acc[i] - lanes_of(parts[m][i], lo + j) * spread[j]
                for i in others:
                    parts[m][i] = acc[i]
                parts[m][t] = rows[m]
            past = t + 1
            while done < len(work) and done * panels < past * len(work):
                work[done]()
                done += 1
        far = [i for i in range(panels) if i not in near]
        if not far:
            continue
        base = window * w
        wide = lax.broadcasted_iota(jnp.int32, (PANEL * len(far), TILE), 1)
        own_lanes = (wide >= base) & (wide < base + window)
        for m in each:
            block = parts[m][groups * w : groups * (w + 1)]
            above, under = base, TILE - base - window
            if above:
                block = [jnp.zeros((above, TILE), F32), *block]
            if under:
                block = [*block, jnp.zeros((under, TILE), F32)]
            bh, bl = split(jnp.concatenate(block, axis=0))
            old = jnp.concatenate([parts[m][i] for i in far], axis=0)
            xh, xl = split(old)
            change = mm(jnp.concatenate([xh, xl], 1), jnp.concatenate([bh, bh], 0)) + mm(xh, bl)
            new = jnp.where(own_lanes, 0.0, old) - change
            for s, i in enumerate(far):
                parts[m][i] = new[PANEL * s : PANEL * (s + 1), :]
    for m in each:
        for g in range(panels):
            refs[m][PANEL * g : PANEL * (g + 1), :] = parts[m][g]


def mm(a, b):
    return jnp.dot(a, b, preferred_element_type=F32)


def split(x):
    hi = x.astype(BF16)
    return hi, (x - hi.astype(F32)).astype(BF16)


def left(x):
    h, l = split(x)
    return jnp.concatenate([h, h, l], 1)


def right(x):
    h, l = split(x)
    return jnp.concatenate([h, l, h], 0)


def dot3(a, b):
    return mm(left(a), right(b))


def dot3_nt(a, b):
    h, l = split(b)
    return lax.dot_general(
        left(a), jnp.concatenate([h, l, h], 1), NT, preferred_element_type=F32
    )


def sweep_inverse(mats, tiles, columns, rows, window):
    count, n, _ = mats.shape
    each = range(count)
    tiles, saved = tiles[:count], tiles[count:]
    last = n // TILE - 1

    def begin(k, m):
        at = pl.multiple_of(k * TILE, TILE)
        here = pl.ds(at, TILE)
        row = lax.broadcasted_iota(jnp.int32, (n, TILE), 0)
        pivot_rows = (row >= at) & (row < at + TILE)
        inverse = saved[m][...]
        scaled = dot3(inverse, mats[m, here, :])
        columns[m] = left(jnp.where(pivot_rows, 0.0, mats[m, :, here]))
        mats[m, :, here] = jnp.zeros((n, TILE), F32)
        mats[m, here, :] = scaled
        mats[m, here, here] = inverse
        rows[m] = right(mats[m, here, :])

    def update(m, c):
        at = slice(c, c + CHUNK)
        mats[m, :, at] = mats[m, :, at] - mm(columns[m], rows[m, :, at])

    work = [functools.partial(update, m, c) for c in range(0, n, CHUNK) for m in each]

    def step(k, carry):
        here = pl.ds(pl.multiple_of(k * TILE, TILE), TILE)
        after = pl.ds(pl.multiple_of((k + 1) * TILE, TILE), TILE)
        for m in each:
            inverse = tiles[m][...]
            saved[m][...] = inverse
            scaled = dot3(inverse, mats[m, here, after])
            tiles[m][...] = mats[m, after, after] - dot3(mats[m, after, here], scaled)
        begins = [functools.partial(begin, k, m) for m in each]
        invert_tiles([tiles[m] for m in each], window, begins + work)
        return carry

    for m in each:
        tiles[m][...] = mats[m, :TILE, :TILE]
    invert_tiles([tiles[m] for m in each], window)
    lax.fori_loop(0, last, step, 0)
    for m in each:
        saved[m][...] = tiles[m][...]
        begin(last, m)
    for item in work:
        item()


def as_column(row):
    n = row.shape[1]
    eye = lax.broadcasted_iota(jnp.int32, (TILE, TILE), 0) == lax.broadcasted_iota(
        jnp.int32, (TILE, TILE), 1
    )
    parts = []
    for t in range(0, n, TILE):
        wide = jnp.broadcast_to(row[:, t : t + TILE], (TILE, TILE))
        parts.append(jnp.sum(jnp.where(eye, wide, 0.0), axis=1, keepdims=True))
    return jnp.concatenate(parts, axis=0)


def diagonal():
    return lax.broadcasted_iota(jnp.int32, (TILE, TILE), 0) == lax.broadcasted_iota(
        jnp.int32, (TILE, TILE), 1
    )


def hours_kernel(
    place, barrier_scale, regularizer, availability, block_rhs, link_mask, state, incoming, message,
    link_in, constraints, border_hbm, border_t_hbm,
    inverses_hbm, kept, lent, solved, avail,
    inverses, border, border_t, scaled, coupled, columns, rows, sems, *tiles,
):
    nb, nv = constraints.shape
    nk = link_in.shape[1]
    loads = [
        pltpu.make_async_copy(border_hbm, border, sems.at[0]),
        pltpu.make_async_copy(border_t_hbm, border_t, sems.at[1]),
    ]
    for load in loads:
        load.start()
    count, second = place[0], place[1] == 1
    two, three = count >= 2, count == 3
    eye = diagonal()

    def early_late(field, at):
        own = [field[s : s + 1, :].astype(F32) for s in range(3)]
        borrowed = message[:, at : at + field.shape[1]]
        early = jnp.where(two, jnp.where(second & three, own[1], own[0]), borrowed)
        early = jnp.where(second, early, own[0])
        late = jnp.where(three, own[2], jnp.where(two, own[1], own[0]))
        late = jnp.where(second, late, jnp.where(two, own[1], borrowed))
        return early, late

    scale = early_late(barrier_scale, 0)
    diag = early_late(regularizer, nv)
    for m in range(HOURS):
        scaled[...] = (constraints[...].astype(F32) * scale[m]).astype(BF16)
        for c in range(0, nb, CHUNK):
            inverses[m, :, c : c + CHUNK] = lax.dot_general(
                scaled[...], constraints[c : c + CHUNK, :], NT, preferred_element_type=F32
            )
        for i in range(0, nb, TILE):
            down = slice(i, i + TILE)
            for j in range(0, i, TILE):
                across = slice(j, j + TILE)
                block = 0.5 * (inverses[m, down, across] + inverses[m, across, down].T)
                inverses[m, down, across] = block
                inverses[m, across, down] = block.T
            block = inverses[m, down, down]
            extra = jnp.where(eye, diag[m][:, down], 0.0)
            inverses[m, down, down] = 0.5 * (block + block.T) + extra
    sweep_inverse(inverses, tiles, columns, rows, PANEL)
    store = pltpu.make_async_copy(inverses, inverses_hbm, sems.at[2])
    store.start()
    own_state = [state[s : s + 1, :] for s in range(3)]
    arrived = incoming[...]
    given = message[:, nv + 3 * nb + nk :]
    early_state = jnp.where(three, own_state[0], jnp.where(two, arrived, given))
    early_state = jnp.where(second, early_state, arrived)
    late_state = jnp.where(three, own_state[1], jnp.where(two, own_state[0], arrived))
    late_state = jnp.where(second, late_state, own_state[0])
    active = early_late(link_mask, nv + 3 * nb)
    linked = jnp.concatenate(
        [active[0] * early_state, active[1] * late_state, jnp.zeros((6, nk), F32)], axis=0
    )
    links = dot3_nt(linked, link_in[...])
    rhs = early_late(block_rhs, nv + 2 * nb)
    available = early_late(availability, nv + nb)
    total = jnp.zeros((1, nb), F32)
    for m in range(HOURS):
        avail[m : m + 1, :] = available[m]
        corrected = as_column(rhs[m] + links[m : m + 1, :])
        y = jnp.sum(corrected * inverses[m], axis=0, keepdims=True)
        solved[m : m + 1, :] = y
        total = total + available[m] * y
    middle = jnp.zeros((nb, nb), F32)
    for m in range(HOURS):
        middle = middle + inverses[m] * as_column(available[m]) * available[m]
    for load in loads:
        load.wait()
    gradient = jnp.sum(as_column(total) * border[...], axis=0, keepdims=True)
    coupled[...] = dot3_nt(middle, border_t[...])
    half = kept.shape[0]

    def put(row, value):
        first = (row < half) == (place[1] == 0)
        at = slice(row % half, row % half + value.shape[0])

        @pl.when(first)
        def _():
            kept[at, :] = value

        @pl.when(jnp.logical_not(first))
        def _():
            lent[at, :] = value

    row = 0
    for i in range(0, nb, TILE):
        part = dot3(border_t[i : i + TILE, :], coupled[:, : i + TILE])
        for j in range(0, i + TILE, TILE):
            put(row, part[:, j : j + TILE])
            row += TILE
    parts = [gradient[:, t * TILE : (t + 1) * TILE] for t in range(nb // TILE)]
    parts.append(jnp.zeros((2 * half - row - len(parts), TILE), F32))
    put(row, jnp.concatenate(parts, axis=0))
    store.wait()


def as_row(column):
    wide = jnp.broadcast_to(column, (TILE, TILE))
    return jnp.sum(jnp.where(diagonal(), wide, 0.0), axis=0, keepdims=True)


def finish_kernel(
    place, mine, other, first_diag, first_rhs, avail, solved, border_hbm, inverses_hbm,
    first_step, slots, sent,
    schur, rhs, heads, border, inverses, sems, tile,
):
    nb = schur.shape[0]
    count = nb // TILE
    half = mine.shape[0]
    loads = [
        pltpu.make_async_copy(border_hbm, border, sems.at[0]),
        pltpu.make_async_copy(inverses_hbm, inverses, sems.at[1]),
    ]
    for load in loads:
        load.start()
    eye = diagonal()

    def get(row, rows):
        at = slice(row % half, row % half + rows)
        return jnp.where((row < half) == (place[1] == 0), mine[at, :], other[at, :])

    row = 0
    for i in range(0, nb, TILE):
        for j in range(0, i + TILE, TILE):
            block = get(row, TILE)
            row += TILE
            if i == j:
                block = block + jnp.where(eye, first_diag[i : i + TILE].reshape(1, TILE), 0.0)
            schur[i : i + TILE, j : j + TILE] = block
    tail = get(row, 8)
    gradient = jnp.concatenate([tail[t : t + 1, :] for t in range(count)], axis=1)
    rhs[...] = as_column(gradient - first_rhs[...].reshape(1, nb))

    def eliminate(k):
        here, below = slice(k * TILE, (k + 1) * TILE), slice((k + 1) * TILE, nb)
        pivot = tile[...]
        column = schur[below, here]
        scaled = dot3(column, pivot)
        factor = left(scaled)
        h, l = split(column)
        across = jnp.concatenate([h, l, h], 1)
        for c in range(0, nb - (k + 1) * TILE, TILE):
            start = (k + 1) * TILE + c
            at = (slice(start, nb), slice(start, start + TILE))
            schur[at] = schur[at] - lax.dot_general(
                factor[c:, :], across[c : c + TILE, :], NT, preferred_element_type=F32
            )
        schur[below, here] = scaled
        own = rhs[here, :]
        heads[k : k + 1, :] = jnp.sum(own * pivot, axis=0, keepdims=True)
        rhs[below, :] = rhs[below, :] - jnp.sum(scaled * as_row(own), axis=1, keepdims=True)

    def step(k, carry):
        for done in range(1, count):
            pl.when(k == done)(functools.partial(eliminate, done - 1))
        here = pl.ds(pl.multiple_of(k * TILE, TILE), TILE)
        tile[...] = schur[here, here]
        invert_tiles([tile], TILE)
        return carry

    lax.fori_loop(0, count, step, 0)
    x = jnp.sum(rhs[nb - TILE :, :] * tile[...], axis=0, keepdims=True)
    found_row, found_column = x, as_column(x)
    for k in range(count - 2, -1, -1):
        below = schur[(k + 1) * TILE :, k * TILE : (k + 1) * TILE]
        x = heads[k : k + 1, :] - jnp.sum(found_column * below, axis=0, keepdims=True)
        found_row = jnp.concatenate([x, found_row], axis=1)
        found_column = jnp.concatenate([as_column(x), found_column], axis=0)
    first_step[...] = found_row.reshape(nb)
    for load in loads:
        load.wait()
    v = jnp.sum(border[...] * found_row, axis=1, keepdims=True)
    steps = []
    for m in range(HOURS):
        w = as_column(avail[m : m + 1, :]) * v
        steps.append(
            solved[m : m + 1, :] - jnp.sum(w * inverses[m], axis=0, keepdims=True)
        )
    early, late = steps
    zero = jnp.zeros_like(early)
    held, second = place[0], place[1] == 1
    two, three = held >= 2, held == 3
    sent[...] = jnp.where(second, early, late)
    slots[0:1, :] = jnp.where(second & jnp.logical_not(two), late, early)
    slots[1:2, :] = jnp.where(two, jnp.where(second & three, early, late), zero)
    slots[2:3, :] = jnp.where(second & three, late, zero)


def message_kernel(
    place, barrier_scale, regularizer, availability, block_rhs, link_mask, primal, link_out,
    state, last, message,
):
    padded = jnp.concatenate([primal[...], jnp.zeros((5, primal.shape[1]), F32)], axis=0)
    states = dot3_nt(padded, link_out[...])
    state[...] = states[:3, :]
    count, second = place[0], place[1] == 1
    last[...] = jnp.where(
        count == 3, states[2:3, :], jnp.where(count == 2, states[1:2, :], states[:1, :])
    )
    at = 0
    for field in (barrier_scale, regularizer, availability, block_rhs, link_mask):
        width = field.shape[1]
        lent = jnp.where(second, field[0:1, :], field[2:3, :])
        message[:, at : at + width] = lent.astype(F32)
        at += width
    message[:, at:] = states[1:2, :]


PARAMS = pltpu.CompilerParams(vmem_limit_bytes=56 * 2**20)


def sweep_scratch(count, n):
    return [
        pltpu.VMEM((count, n, 3 * TILE), BF16),
        pltpu.VMEM((count, 3 * TILE, n), BF16),
        pltpu.SemaphoreType.DMA((3,)),
        *(pltpu.VMEM((TILE, TILE), F32) for _ in range(2 * count)),
    ]


def spaces(count, scalar, remote):
    return [
        pl.BlockSpec(
            memory_space=pltpu.SMEM if k in scalar else pl.ANY if k in remote else pltpu.VMEM
        )
        for k in range(count)
    ]


def summed_over_chips(array):
    rows, width = array.shape
    chips = lax.axis_size(CHIPS)
    pieces = array.reshape(chips, rows // chips, width)
    piece = lax.all_to_all(pieces, CHIPS, 0, 0, tiled=True).sum(axis=0)
    spread = jnp.broadcast_to(piece[None], (chips, *piece.shape))
    return lax.all_to_all(spread, CHIPS, 0, 0, tiled=True).reshape(rows, width)


def on_device(
    barrier_scale, regularizer, availability, block_rhs, primal, link_mask, counts,
    constraints, border, link_out, link_in, first_diag, first_rhs,
):
    nb, nv = constraints.shape
    count = counts[0]
    core = lax.axis_index(CORE)
    devices = lax.axis_size(GRP_BLK)
    pair = [(0, 1), (1, 0)]
    place = jnp.stack([count, core])
    nk = link_in.shape[1]
    state, last, lent = pl.pallas_call(
        message_kernel,
        out_shape=(
            jax.ShapeDtypeStruct((3, nk), F32),
            jax.ShapeDtypeStruct((1, nk), F32),
            jax.ShapeDtypeStruct((1, nv + 3 * nb + 2 * nk), F32),
        ),
        in_specs=spaces(8, (0,), ()),
        compiler_params=PARAMS,
        name="message",
    )(place, barrier_scale, regularizer, availability, block_rhs, link_mask, primal, link_out)
    incoming = lax.ppermute(last, GRP_BLK, [(d, d + 1) for d in range(devices - 1)])
    message = lax.ppermute(lent, CORE, pair)
    packed_rows = (nb // TILE) * (nb // TILE + 1) // 2 * TILE + 8
    packed_rows = -(-packed_rows // (devices * 8)) * devices * 8
    square = pltpu.VMEM((nb, nb), F32)
    pairs = pltpu.VMEM((HOURS, nb, nb), F32)
    inverses, kept, sent, solved, avail = pl.pallas_call(
        hours_kernel,
        out_shape=(
            jax.ShapeDtypeStruct((HOURS, nb, nb), F32),
            jax.ShapeDtypeStruct((packed_rows // 2, TILE), F32),
            jax.ShapeDtypeStruct((packed_rows // 2, TILE), F32),
            jax.ShapeDtypeStruct((HOURS, nb), F32),
            jax.ShapeDtypeStruct((HOURS, nb), F32),
        ),
        in_specs=spaces(13, (0,), (11, 12)),
        out_specs=spaces(5, (), (0,)),
        scratch_shapes=[
            pairs, square, square, pltpu.VMEM((nb, nv), BF16), square, *sweep_scratch(HOURS, nb)
        ],
        compiler_params=PARAMS,
        name="hours",
    )(
        place, barrier_scale, regularizer, availability, block_rhs, link_mask, state, incoming,
        message, link_in, constraints, border, border.T,
    )
    mine = summed_over_chips(kept + lax.ppermute(sent, CORE, pair))
    other = lax.ppermute(mine, CORE, pair)
    first_step, slots, sent = pl.pallas_call(
        finish_kernel,
        out_shape=(
            jax.ShapeDtypeStruct((nb,), F32),
            jax.ShapeDtypeStruct((3, nb), F32),
            jax.ShapeDtypeStruct((1, nb), F32),
        ),
        in_specs=spaces(9, (0,), (7, 8)),
        scratch_shapes=[
            square, pltpu.VMEM((nb, 1), F32), pltpu.VMEM((8, TILE), F32), square, pairs,
            pltpu.SemaphoreType.DMA((2,)), pltpu.VMEM((TILE, TILE), F32),
        ],
        compiler_params=PARAMS,
        name="finish",
    )(place, mine, other, first_diag, first_rhs, avail, solved, border, inverses)
    returned = lax.ppermute(sent, CORE, pair)
    slot = jnp.arange(3, dtype=jnp.int32)[:, None]
    borrowed_slot = jnp.where(count == 3, 2 - 2 * core, -1)
    return jnp.where(slot == borrowed_slot, returned, slots), first_step


def solution(mesh):
    split_mesh = Mesh(mesh.devices.reshape(mesh.shape["grp"], 4, 4, 2), GRP_BLK)
    whole = P(GRP_BLK, None)
    placed = (whole,) * 6 + (P(GRP_BLK),) + (P(),) * 6
    return jax.shard_map(
        on_device, mesh=split_mesh, in_specs=placed, out_specs=(whole, P()), check_vma=False
    )
```
